512 devices in a mesh: prow: 16 (over z_hi, y), pcol: 32 (over z_lo, x, core).
Axes of the slice: x: 4, y: 8, z: 8 (z_hi: 2, z_lo: 4; z = z_hi * 4 + z_lo), core: 2. Of those that a mesh axis runs over, the one named last changes fastest.
Arguments:
- latent: bfloat16 [64, 128, 1280], P('prow', 'pcol'), may hold values from -8 to 8
- norm_scale: float32 [3, 1280], replicated, may hold values from 0.25 to 1.75
- norm_shift: float32 [3, 1280], replicated, may hold values from -3 to 3
- time_shift: float32 [1280], replicated, may hold values from -4 to 4
- conv_bias: float32 [2, 1280], replicated, may hold values from -3 to 3
- conv_one: bfloat16 [3, 3, 1280, 1280], P(None, None, 'prow'), may hold values from -0.0546875 to 0.0546875
- conv_two: bfloat16 [3, 3, 1280, 1280], P(None, None, 'prow'), may hold values from -0.0546875 to 0.0546875
- w_qkv: bfloat16 [3072, 1280], P('prow'), may hold values from -0.3125 to 0.3125
- w_out: bfloat16 [1280, 1024], P('prow'), may hold values from -0.1875 to 0.1875
- stale_kv: bfloat16 [64, 128, 16, 128], P(None, 'pcol', 'prow'), may hold values from -36 to 36
Outputs:
- next_latent: bfloat16 [64, 128, 1280], P('prow', 'pcol')
- fresh_kv: bfloat16 [64, 128, 16, 128], P(None, 'pcol', 'prow')
The draws below stay inside these ranges and needn't reach their ends.
All inputs are finite; a program needn't handle non-finite values.
Results may differ from the reference program's by a relative error of at most 0.028.
Values may be sent and summed in bfloat16 or wider, within the bound.
No kernel may reach another device: no remote copies, remote signals or barrier semaphores. Data moves between devices by JAX's collectives and lax.ppermute only.
A program may use at most 64 MiB of HBM per device.

```python
import jax
import jax.numpy as jnp
from jax import lax

C = 1280
GROUPS = 32
HEAD = 64
PC = 4
HEADS = 16
LH = 64
LW = 128
N_PCOL = 32


def draw_latent(key, part):
    first = jax.random.fold_in(jax.random.fold_in(key, 11), 0)
    rows = jnp.arange(LH, dtype=jnp.float32)[:, None] / LH
    cols = jnp.arange(LW, dtype=jnp.float32)[None, :] / LW
    ramp = (3.0 ** (0.5 * (rows + cols)))[:, :, None]
    value = jax.random.normal(first, (LH, LW, C), jnp.float32) * ramp * 0.6
    return jnp.clip(value, -8.0, 8.0).astype(jnp.bfloat16)


def draw_stale_kv(key, part):
    parts = jax.random.split(jax.random.fold_in(key, 23), 1)
    shape = (LH, LW, HEADS, 2 * HEAD)
    base = jax.random.normal(parts[0], shape, jnp.float32) * 1.7
    return jnp.clip(base, -36.0, 36.0).astype(jnp.bfloat16)


def level_of(key, shape, cuts, smallest, largest):
    level, own = 1.0, jax.random.fold_in(key, 6)
    for axis_at, blocks in cuts:
        steps = jnp.exp(jax.random.uniform(jax.random.fold_in(own, axis_at), (blocks,), jnp.float32, smallest / len(cuts), largest / len(cuts)))
        level = level * jnp.repeat(steps, shape[axis_at] // blocks).reshape([-1 if axis == axis_at else 1 for axis in range(len(shape))])
    return level


def scatter_about(stream_key, dims, spread, bound, cuts=(), kind=jnp.bfloat16):
    drawn = spread * jax.random.normal(stream_key, dims, jnp.float32)
    if cuts:
        drawn = drawn * level_of(stream_key, dims, cuts, -0.22, 0.18)
    return jnp.clip(drawn, -bound, bound).astype(kind)


def setup_inputs(seed: int = 0) -> dict:
    key_of = jax.random.split(jax.random.key(seed), 11)
    return {
        "latent": draw_latent(jax.random.fold_in(key_of[10], 71), 0),
        "norm_scale": jnp.clip(1.0 + 0.15 * jax.random.normal(key_of[1], (3, C), jnp.float32), 0.25, 1.75),
        "norm_shift": scatter_about(key_of[2], (3, C), 0.5, 3.0, (), jnp.float32),
        "time_shift": scatter_about(key_of[3], (C,), 1.0, 4.0, (), jnp.float32),
        "conv_bias": scatter_about(key_of[4], (2, C), 0.5, 3.0, (), jnp.float32),
        "conv_one": scatter_about(key_of[5], (3, 3, C, C), (9 * C) ** -0.5, 0.0546875, ((2, 16),)),
        "conv_two": scatter_about(key_of[6], (3, 3, C, C), (9 * C) ** -0.5, 0.0546875, ((2, 16),)),
        "w_qkv": scatter_about(key_of[7], (HEADS * 3 * HEAD, C), (C // 3) ** -0.5, 0.3125, ((0, 16),)),
        "w_out": scatter_about(key_of[8], (C, HEADS * HEAD), (HEADS * HEAD) ** -0.5, 0.1875, ((0, 16),)),
        "stale_kv": draw_stale_kv(jax.random.fold_in(key_of[10], 71), 0),
    }


EPSILON = 1e-05

def group_norm(field, scale, shift):
    grouped = field.reshape(LH * LW, GROUPS, C // GROUPS)
    average = lax.optimization_barrier(jnp.mean(grouped, axis=(0, 2)))
    centered = grouped - average[None, :, None]
    variance = lax.optimization_barrier(jnp.mean(centered * centered, axis=(0, 2)))
    normed = centered * lax.rsqrt(variance + EPSILON)[None, :, None]
    return normed.reshape(LH, LW, C) * scale + shift

def convolve(field, weight):
    padded = jnp.pad(field, ((1, 1), (1, 1), (0, 0)))
    taps = [padded[row_tap:row_tap + LH, col_tap:col_tap + LW, :] for row_tap in range(3) for col_tap in range(3)]
    stacked = jnp.concatenate(taps, axis=-1).reshape(LH * LW, 9 * C)
    matrix = jnp.transpose(weight, (0, 1, 3, 2)).reshape(9 * C, C)
    result = jnp.dot(stacked, matrix, preferred_element_type=jnp.float32)
    return result.reshape(LH, LW, C)

def reference(latent, norm_scale, norm_shift, time_shift, conv_bias, conv_one, conv_two, w_qkv, w_out, stale_kv):
    inputs = latent.astype(jnp.float32)
    first_act = jax.nn.silu(group_norm(inputs, norm_scale[0], norm_shift[0])).astype(jnp.bfloat16)
    first_conv = convolve(first_act, conv_one) + conv_bias[0] + time_shift
    second_act = jax.nn.silu(group_norm(first_conv, norm_scale[1], norm_shift[1])).astype(jnp.bfloat16)
    resnet_out = (inputs + convolve(second_act, conv_two) + conv_bias[1]).astype(jnp.bfloat16)
    attn_in = group_norm(resnet_out.astype(jnp.float32), norm_scale[2], norm_shift[2]).astype(jnp.bfloat16)
    qkv = jnp.dot(attn_in.reshape(LH * LW, C), w_qkv.T, preferred_element_type=jnp.float32).astype(jnp.bfloat16)
    qkv = qkv.reshape(LH, LW, HEADS, 3, HEAD)
    queries = qkv[:, :, :, 0, :]
    fresh_kv = jnp.concatenate([qkv[:, :, :, 1, :], qkv[:, :, :, 2, :]], axis=-1)
    scale = HEAD ** (-0.5)

    def strip_attend(strip):
        start = (strip * PC).astype(jnp.int32)
        strip_queries = lax.dynamic_slice_in_dim(queries, start, PC, 1).reshape(LH * PC, HEADS, HEAD)
        fresh_strip = lax.dynamic_slice_in_dim(fresh_kv, start, PC, 1)
        pairs = lax.dynamic_update_slice_in_dim(stale_kv, fresh_strip, start, 1).reshape(LH * LW, HEADS, 2 * HEAD)
        keys = pairs[:, :, :HEAD].astype(jnp.float32)
        values = pairs[:, :, HEAD:].astype(jnp.float32)
        scores = jnp.einsum('qhd,khd->hqk', strip_queries.astype(jnp.float32), keys) * scale
        highest = lax.optimization_barrier(jnp.max(scores, axis=-1))
        weights = jnp.exp(scores - highest[..., None])
        denominator = lax.optimization_barrier(jnp.sum(weights, axis=-1))
        probs = weights.astype(jnp.bfloat16).astype(jnp.float32)
        weighted = jnp.einsum('hqk,khd->qhd', probs, values)
        return (weighted / denominator.T[..., None]).astype(jnp.bfloat16)
    attended = lax.map(strip_attend, jnp.arange(N_PCOL, dtype=jnp.int32))
    attended = attended.reshape(N_PCOL, LH, PC, HEADS * HEAD).transpose(1, 0, 2, 3).reshape(LH * LW, HEADS * HEAD)
    added = jnp.dot(attended, w_out.T, preferred_element_type=jnp.float32)
    next_latent = (resnet_out.astype(jnp.float32).reshape(LH * LW, C) + added).astype(jnp.bfloat16).reshape(LH, LW, C)
    return (next_latent, fresh_kv)
```

```python
import functools

import jax
import jax.numpy as jnp
from jax import lax
from jax.experimental import pallas as pl
from jax.experimental.pallas import tpu as pltpu
from jax.sharding import Mesh
from jax.sharding import PartitionSpec as P

GROUPS = 32
HEAD = 64
PROW = ("prow_0", "prow_1")
PCOL = ("pcol_0", "pcol_1", "pcol_2")
EPSILON = 1e-05
F32 = jnp.float32
BF16 = jnp.bfloat16

C = 1280
GC = C // GROUPS
NP = 16
NS = 32
LR = 64
PC = 4
CELLS = LR * PC
OC = C // NP
POPULATION = float(LR * PC * NS * GC)


def iota(shape, dim):
    return lax.broadcasted_iota(jnp.int32, shape, dim)


def one_hot(mask, dtype):
    return jnp.where(mask, 1.0, 0.0).astype(dtype)


def nt(left, right, precision=None):
    return lax.dot_general(
        left, right, (((1,), (1,)), ((), ())), precision=precision, preferred_element_type=F32
    )


def nn(left, right, precision=None):
    return lax.dot_general(
        left, right, (((1,), (0,)), ((), ())), precision=precision, preferred_element_type=F32
    )


def strip_order():
    o = iota((CELLS, CELLS), 0)
    i = iota((CELLS, CELLS), 1)
    return one_hot((o % LR) * PC + o // LR == i, BF16)


def cell_order():
    o = iota((CELLS, CELLS), 1)
    i = iota((CELLS, CELLS), 0)
    return one_hot((o % LR) * PC + o // LR == i, BF16)


def moments(sums_ref):
    sums = jnp.sum(sums_ref[...], axis=0)
    mean = sums / POPULATION
    square = pltpu.roll(mean, 128 - GROUPS, 1)
    return mean, lax.rsqrt(jnp.maximum(square - mean * mean, 0.0) + EPSILON)


def silu(v):
    return v / (1.0 + jnp.exp(-v))


def stats_cells_kernel(x_ref, out_ref):
    x = x_ref[...].astype(F32)
    first = jnp.sum(x, axis=0, keepdims=True)
    second = jnp.sum(x * x, axis=0, keepdims=True)
    both = jnp.concatenate([first, second, jnp.zeros((6, C), F32)], axis=0)
    groups = one_hot(iota((C, 128), 0) // GC == iota((C, 128), 1), F32)
    reduced = nn(both, groups, lax.Precision.HIGHEST)
    row = reduced[0:1, :] + pltpu.roll(reduced, GROUPS, 1)[1:2, :]
    out_ref[...] = jnp.broadcast_to(row[None], out_ref.shape)


def stats_channels_kernel(x_ref, out_ref):
    firsts, seconds = [], []
    for pair in range(NP):
        x = x_ref[OC * pair : OC * (pair + 1), :].astype(F32)
        y = x * x
        x = x[:, :128] + x[:, 128:]
        y = y[:, :128] + y[:, 128:]
        for half in range(2):
            firsts.append(jnp.sum(x[GC * half : GC * (half + 1)], axis=0, keepdims=True))
            seconds.append(jnp.sum(y[GC * half : GC * (half + 1)], axis=0, keepdims=True))
    first = jnp.sum(jnp.concatenate(firsts, axis=0), axis=1, keepdims=True)
    second = jnp.sum(jnp.concatenate(seconds, axis=0), axis=1, keepdims=True)
    group = iota((GROUPS, 128), 0)
    lane = iota((GROUPS, 128), 1)
    spread = jnp.where(group == lane, first, 0.0) + jnp.where(group + GROUPS == lane, second, 0.0)
    out_ref[...] = jnp.broadcast_to(jnp.sum(spread, axis=0, keepdims=True)[None], out_ref.shape)


def conv_combine(products, mid_ref, to_left_ref, to_right_ref):
    lane = iota((OC, CELLS), 1)
    row = lane % LR

    def tap(a, b):
        at = (3 * a + b) * OC
        return products[at : at + OC, :]

    def rows_summed(b):
        above = jnp.where(row > 0, pltpu.roll(tap(0, b), 1, 1), 0.0)
        below = jnp.where(row < LR - 1, pltpu.roll(tap(2, b), CELLS - 1, 1), 0.0)
        return tap(1, b) + above + below

    before = rows_summed(0)
    after = rows_summed(2)
    to_right_ref[...] = before[:, CELLS - LR :]
    to_left_ref[...] = after[:, :LR]
    mid_ref[...] = (
        rows_summed(1)
        + jnp.where(lane >= LR, pltpu.roll(before, LR, 1), 0.0)
        + jnp.where(lane < CELLS - LR, pltpu.roll(after, CELLS - LR, 1), 0.0)
    )


def conv_cells_kernel(
    at_ref, x_ref, sums_ref, scale_ref, shift_ref, w_ref, mid_ref, left_ref, right_ref, own_ref
):
    mean, rstd = moments(sums_ref)
    both = jnp.concatenate([mean, rstd, jnp.zeros((6, 128), F32)], axis=0)
    groups = one_hot(iota((128, C), 1) // GC == iota((128, C), 0), F32)
    spread = nn(both, groups, lax.Precision.HIGHEST)
    gain = spread[1:2, :] * scale_ref[0:1, :]
    offset = shift_ref[0:1, :] - spread[0:1, :] * gain
    cells = nn(strip_order(), x_ref[...])
    pick = one_hot(iota((OC, C), 1) == iota((OC, C), 0) + at_ref[0] * OC, BF16)
    own_ref[...] = nt(pick, cells.astype(BF16))
    act = silu(cells * gain + offset).astype(BF16)
    conv_combine(nt(w_ref[...], act), mid_ref, left_ref, right_ref)


def normed_channels(x_ref, sums_ref, cols_ref, col, act_ref, apply):
    mean, rstd = moments(sums_ref)
    for pair in range(NP):
        parts = []
        for half in range(2):
            g = 2 * pair + half
            rows = slice(GC * g, GC * (g + 1))
            gain = cols_ref[rows, col : col + 1] * rstd[:, g : g + 1]
            offset = cols_ref[rows, col + 1 : col + 2] - mean[:, g : g + 1] * gain
            parts.append((gain, offset))
        gain = jnp.concatenate([parts[0][0], parts[1][0]], axis=0)
        offset = jnp.concatenate([parts[0][1], parts[1][1]], axis=0)
        rows = slice(OC * pair, OC * (pair + 1))
        act_ref[rows, :] = apply(x_ref[rows, :].astype(F32) * gain + offset).astype(BF16)


def conv_channels_kernel(x_ref, sums_ref, cols_ref, w_ref, mid_ref, left_ref, right_ref, act_ref):
    normed_channels(x_ref, sums_ref, cols_ref, 0, act_ref, silu)
    conv_combine(nn(w_ref[...], act_ref[...]), mid_ref, left_ref, right_ref)


def finish_kernel(which, at_ref, mid_ref, from_left_ref, from_right_ref, bias_ref, extra_ref, out_ref):
    row = bias_ref[which : which + 1, :]
    if which == 0:
        row = row + extra_ref[...]
    pick = iota((OC, C), 1) == iota((OC, C), 0) + at_ref[0] * OC
    bias = jnp.sum(jnp.where(pick, row, 0.0), axis=1, keepdims=True)
    sides = jnp.concatenate(
        [from_left_ref[...], jnp.zeros((OC, CELLS - 2 * LR), F32), from_right_ref[...]], axis=1
    )
    total = mid_ref[...] + sides + bias
    if which == 1:
        total = extra_ref[...] + total
    out_ref[...] = jnp.broadcast_to(total.astype(BF16)[None], out_ref.shape)


def attention_kernel(
    at_ref, x_ref, sums_ref, cols_ref, w_ref, pairs_ref, att_ref, fresh_ref, own_ref, act_ref
):
    normed_channels(x_ref, sums_ref, cols_ref, 2, act_ref, lambda v: v)
    mapped = nn(w_ref[...], act_ref[...])
    queries = jnp.transpose(mapped[:HEAD]).astype(BF16)
    fresh = jnp.transpose(mapped[HEAD:]).astype(BF16)
    queries = (queries.astype(F32) * HEAD ** (-0.5)).astype(BF16)
    queries = jnp.concatenate([queries, jnp.zeros((CELLS, HEAD), BF16)], axis=1)
    order = cell_order()
    fresh_ref[...] = nn(order, fresh).astype(BF16)
    pick = one_hot(
        iota((NP, CELLS), 1)
        == (iota((NP, CELLS), 0) % PC) * LR + at_ref[0] * PC + iota((NP, CELLS), 0) // PC,
        BF16,
    )
    own_ref[...] = nt(pick, x_ref[...])
    chunk = 4
    highest = jnp.full((CELLS, 1), -jnp.inf, F32)
    denominator = jnp.zeros((CELLS, 1), F32)
    weighted = jnp.zeros((CELLS, 2 * HEAD), F32)
    for step in range(NS // chunk):
        blocks = []
        for k in range(chunk):
            strip = chunk * step + k
            blocks.append(jnp.where(at_ref[1] == strip, fresh, pairs_ref[strip]))
        pairs = jnp.concatenate(blocks, axis=0)
        scores = nt(queries, pairs)
        raised = jnp.maximum(highest, jnp.max(scores, axis=1, keepdims=True))
        factor = jnp.exp(highest - raised)
        weights = jnp.exp(scores - raised)
        denominator = denominator * factor + jnp.sum(weights, axis=1, keepdims=True)
        weighted = weighted * factor + nn(weights.astype(BF16), pairs)
        highest = raised
    attended = (weighted / denominator).astype(BF16)
    att_ref[...] = nn(order, attended)[:, HEAD:].astype(BF16)


def output_kernel(att_ref, w_ref, own_ref, out_ref):
    att = jnp.concatenate([att_ref[k] for k in range(NP)], axis=1)
    out_ref[...] = (own_ref[...] + nt(att, w_ref[...])).astype(BF16)


def call(kernel, name, outs, scalars=0, scratch=()):
    def run(*args):
        specs = [pl.BlockSpec(memory_space=pltpu.SMEM)] * scalars
        specs += [pl.BlockSpec(memory_space=pltpu.VMEM)] * (len(args) - scalars)
        return pl.pallas_call(
            kernel,
            out_shape=[jax.ShapeDtypeStruct(*out) for out in outs],
            in_specs=specs,
            out_specs=[pl.BlockSpec(memory_space=pltpu.VMEM)] * len(outs),
            scratch_shapes=list(scratch),
            name=name,
        )(*args)

    return run


def to_every(copies, axis):
    return lax.all_to_all(copies, axis, split_axis=0, concat_axis=0, tiled=True)


def beside(value, step):
    pairs = [(i, i + step) for i in range(NS) if 0 <= i + step < NS]
    return lax.ppermute(value, PCOL, pairs)


def shards(
    latent,
    norm_scale,
    norm_shift,
    time_shift,
    conv_bias,
    conv_one,
    conv_two,
    w_qkv,
    w_out,
    stale_kv,
):
    at = jnp.stack([lax.axis_index(PROW), lax.axis_index(PCOL)]).astype(jnp.int32)
    cols = jnp.stack([norm_scale[1], norm_shift[1], norm_scale[2], norm_shift[2]]).T
    pairs = lax.all_gather(stale_kv.reshape(CELLS, 2 * HEAD), PCOL, axis=0)
    w_out_all = lax.all_gather(w_out, PROW, axis=0, tiled=True)
    sums_out = ((NS, 1, 128), F32)
    conv_out = [((OC, CELLS), F32), ((OC, LR), F32), ((OC, LR), F32)]
    act = pltpu.VMEM((C, CELLS), BF16)

    patch = latent.reshape(NP, C)
    strip = to_every(jnp.broadcast_to(patch, (NP, NP, C)), PROW).reshape(CELLS, C)
    (sums,) = call(stats_cells_kernel, "stats0", [sums_out])(strip)
    sums = to_every(sums, PCOL)
    mid, left, right, own = call(
        conv_cells_kernel, "conv1", conv_out + [((OC, CELLS), F32)], scalars=1
    )(at, strip, sums, norm_scale, norm_shift, conv_one.reshape(9 * OC, C))
    (block,) = call(
        functools.partial(finish_kernel, 0), "finish1", [((NP, OC, CELLS), BF16)], scalars=1
    )(at, mid, beside(right, 1), beside(left, -1), conv_bias, time_shift.reshape(1, C))

    field = to_every(block, PROW).reshape(C, CELLS)
    (sums,) = call(stats_channels_kernel, "stats1", [sums_out])(field)
    sums = to_every(sums, PCOL)
    mid, left, right = call(conv_channels_kernel, "conv2", conv_out, scratch=[act])(
        field, sums, cols, conv_two.reshape(9 * OC, C)
    )
    (block,) = call(
        functools.partial(finish_kernel, 1), "finish2", [((NP, OC, CELLS), BF16)], scalars=1
    )(at, mid, beside(right, 1), beside(left, -1), conv_bias, own)

    field = to_every(block, PROW).reshape(C, CELLS)
    (sums,) = call(stats_channels_kernel, "stats2", [sums_out])(field)
    sums = to_every(sums, PCOL)
    attended, fresh, resnet_own = call(
        attention_kernel,
        "attention",
        [((CELLS, HEAD), BF16), ((CELLS, 2 * HEAD), BF16), ((NP, C), F32)],
        scalars=1,
        scratch=[act],
    )(at, field, sums, cols, w_qkv, pairs)
    heads = to_every(attended.reshape(NP, NP, HEAD), PROW)
    (out,) = call(output_kernel, "output", [((NP, C), BF16)])(heads, w_out_all, resnet_own)
    return out.reshape(latent.shape), fresh.reshape(LR, PC, 1, 2 * HEAD)


def solution(mesh):
    torus = Mesh(
        mesh.devices.reshape(2, 8, 4, 4, 2), ("prow_0", "prow_1", "pcol_0", "pcol_1", "pcol_2")
    )
    in_specs = (
        P(PROW, PCOL, None),
        P(),
        P(),
        P(),
        P(),
        P(None, None, PROW, None),
        P(None, None, PROW, None),
        P(PROW, None),
        P(PROW, None),
        P(None, PCOL, PROW, None),
    )
    out_specs = (P(PROW, PCOL, None), P(None, PCOL, PROW, None))
    return jax.shard_map(
        shards, mesh=torus, in_specs=in_specs, out_specs=out_specs, check_vma=False
    )
```

```python
import functools

import jax
import jax.numpy as jnp
from jax import lax
from jax.experimental import pallas as pl
from jax.experimental.pallas import tpu as pltpu
from jax.sharding import Mesh
from jax.sharding import PartitionSpec as P

GROUPS = 32
HEAD = 64
PROW = ("prow_0", "prow_1")
PCOL = ("pcol_0", "pcol_1", "pcol_2")
EPSILON = 1e-05
F32 = jnp.float32
BF16 = jnp.bfloat16

C = 1280
GC = C // GROUPS
NP = 16
NS = 32
LR = 64
PC = 4
CELLS = LR * PC
OC = C // NP
POPULATION = float(LR * PC * NS * GC)


def iota(shape, dim):
    return lax.broadcasted_iota(jnp.int32, shape, dim)


def one_hot(mask, dtype):
    return jnp.where(mask, 1.0, 0.0).astype(dtype)


def nt(left, right, precision=None):
    return lax.dot_general(
        left, right, (((1,), (1,)), ((), ())), precision=precision, preferred_element_type=F32
    )


def nn(left, right, precision=None):
    return lax.dot_general(
        left, right, (((1,), (0,)), ((), ())), precision=precision, preferred_element_type=F32
    )


def strip_order():
    o = iota((CELLS, CELLS), 0)
    i = iota((CELLS, CELLS), 1)
    return one_hot((o % LR) * PC + o // LR == i, BF16)


def cell_order():
    o = iota((CELLS, CELLS), 1)
    i = iota((CELLS, CELLS), 0)
    return one_hot((o % LR) * PC + o // LR == i, BF16)


ROWS = OC // 5 * C // 128
PIECE = 48
BLOCK = ROWS + PIECE


def moments(sums_ref):
    sums = jnp.sum(sums_ref[...], axis=0)
    mean = sums / POPULATION
    square = pltpu.roll(mean, 128 - GROUPS, 1)
    return mean, lax.rsqrt(jnp.maximum(square - mean * mean, 0.0) + EPSILON)


def silu(v):
    return v / (1.0 + jnp.exp(-v))


def pack_kernel(latent_ref, w_ref, out_ref):
    rows = [latent_ref[r].astype(F32) for r in range(PC)]
    patch = jnp.concatenate(rows, axis=0).astype(BF16)
    for j in range(C // 128):
        chunk = patch[:, 128 * j : 128 * (j + 1)]
        out_ref[:, NP * j : NP * (j + 1), :] = jnp.broadcast_to(chunk[None], (NP, NP, 128))
    lane = iota((PIECE, 128), 1)
    for k in range(NP // 2):
        w = w_ref[:, 128 * k : 128 * (k + 1)].astype(F32)
        turned = pltpu.roll(w, HEAD, 1)
        blank = jnp.zeros((2 * PIECE - OC, 128), F32)

        def halves(left, right):
            low = jnp.concatenate([right[PIECE:], blank], axis=0)
            return jnp.where(lane < HEAD, left[:PIECE], low).astype(BF16)

        out_ref[2 * k, ROWS:, :] = halves(w, turned)
        out_ref[2 * k + 1, ROWS:, :] = halves(turned, w)


def unpack_kernel(block_ref, out_ref):
    lane = iota((PIECE, 128), 1)
    for p in range(NP):
        piece = block_ref[p, ROWS:, :].astype(F32)
        high = jnp.where(lane >= HEAD, pltpu.roll(piece, HEAD, 1), 0.0)
        low = jnp.where(lane >= HEAD, piece, 0.0)
        both = jnp.concatenate([high, low[: OC - PIECE]], axis=0)
        out_ref[OC * p : OC * (p + 1), :] = both.astype(BF16)


def columns_kernel(at_ref, scale_ref, shift_ref, bias_ref, time_ref, out_ref):
    pick = iota((OC, C), 1) == iota((OC, C), 0) + at_ref[0] * OC
    lane = iota((OC, 128), 1)
    total = jnp.zeros((OC, 128), F32)
    rows = [
        bias_ref[0:1, :] + time_ref[...],
        scale_ref[1:2, :],
        shift_ref[1:2, :],
        bias_ref[1:2, :],
        scale_ref[2:3, :],
        shift_ref[2:3, :],
    ]
    for k, row in enumerate(rows):
        col = jnp.sum(jnp.where(pick, row, 0.0), axis=1, keepdims=True)
        total = jnp.where(lane == k, col, total)
    out_ref[...] = total


def stats_cells_kernel(block_ref, out_ref):
    firsts, seconds = [], []
    for j in range(C // 128):
        x = block_ref[:, NP * j : NP * (j + 1), :].astype(F32).reshape(CELLS, 128)
        firsts.append(jnp.sum(x, axis=0, keepdims=True))
        seconds.append(jnp.sum(x * x, axis=0, keepdims=True))
    first = jnp.concatenate(firsts, axis=1)
    second = jnp.concatenate(seconds, axis=1)
    both = jnp.concatenate([first, second, jnp.zeros((6, C), F32)], axis=0)
    groups = one_hot(iota((C, 128), 0) // GC == iota((C, 128), 1), F32)
    reduced = nn(both, groups, lax.Precision.HIGHEST)
    row = reduced[0:1, :] + pltpu.roll(reduced, GROUPS, 1)[1:2, :]
    out_ref[...] = jnp.broadcast_to(row[None], out_ref.shape)


def conv_combine(products, mid_ref, to_left_ref, to_right_ref):
    lane = iota((OC, CELLS), 1)
    row = lane % LR

    def tap(a, b):
        at = (3 * a + b) * OC
        return products[at : at + OC, :]

    def rows_summed(b):
        above = jnp.where(row > 0, pltpu.roll(tap(0, b), 1, 1), 0.0)
        below = jnp.where(row < LR - 1, pltpu.roll(tap(2, b), CELLS - 1, 1), 0.0)
        return tap(1, b) + above + below

    before = rows_summed(0)
    after = rows_summed(2)
    to_right_ref[...] = before[:, CELLS - LR :]
    to_left_ref[...] = after[:, :LR]
    mid_ref[...] = (
        rows_summed(1)
        + jnp.where(lane >= LR, pltpu.roll(before, LR, 1), 0.0)
        + jnp.where(lane < CELLS - LR, pltpu.roll(after, CELLS - LR, 1), 0.0)
    )


def conv_cells_kernel(
    at_ref, block_ref, sums_ref, scale_ref, shift_ref, w_ref, mid_ref, left_ref, right_ref, own_ref
):
    mean, rstd = moments(sums_ref)
    both = jnp.concatenate([mean, rstd, jnp.zeros((6, 128), F32)], axis=0)
    groups = one_hot(iota((128, C), 1) // GC == iota((128, C), 0), F32)
    spread = nn(both, groups, lax.Precision.HIGHEST)
    gain = spread[1:2, :] * scale_ref[0:1, :]
    offset = shift_ref[0:1, :] - spread[0:1, :] * gain
    chunks = [
        block_ref[:, NP * j : NP * (j + 1), :].reshape(CELLS, 128) for j in range(C // 128)
    ]
    cells = nn(strip_order(), jnp.concatenate(chunks, axis=1))
    pick = one_hot(iota((OC, C), 1) == iota((OC, C), 0) + at_ref[0] * OC, BF16)
    own_ref[...] = nt(pick, cells.astype(BF16))
    act = silu(cells * gain + offset).astype(BF16)
    conv_combine(nt(w_ref[...], act), mid_ref, left_ref, right_ref)


def conv_channels_kernel(x_ref, w_ref, mid_ref, left_ref, right_ref):
    conv_combine(nn(w_ref[...], x_ref[...]), mid_ref, left_ref, right_ref)


def whole(x):
    return jnp.sum(jnp.sum(x, axis=0, keepdims=True), axis=1, keepdims=True)


def finish_kernel(which, mid_ref, from_left_ref, from_right_ref, cols_ref, *refs):
    total_ref, sums_ref = refs[-2:]
    sides = jnp.concatenate(
        [from_left_ref[...], jnp.zeros((OC, CELLS - 2 * LR), F32), from_right_ref[...]], axis=1
    )
    total = mid_ref[...] + sides + cols_ref[:, 3 * which : 3 * which + 1]
    if which == 1:
        total = refs[0][...] + total
        total_ref[...] = total.astype(BF16)
        total = total.astype(BF16).astype(F32)
    else:
        total_ref[...] = total
    lane = iota((1, 128), 1)
    row = jnp.zeros((1, 128), F32)
    for k in range(2):
        half = total[GC * k : GC * (k + 1)]
        row = jnp.where(lane == k, whole(half), row)
        row = jnp.where(lane == k + GROUPS, whole(half * half), row)
    sums_ref[...] = jnp.broadcast_to(row[None], sums_ref.shape)


def norm_kernel(which, total_ref, sums_ref, cols_ref, out_ref):
    mean, rstd = moments(sums_ref)
    upper = iota((OC, 1), 0) < GC
    gain = jnp.where(upper, rstd[:, 0:1], rstd[:, 1:2]) * cols_ref[:, 3 * which + 1 : 3 * which + 2]
    shift = cols_ref[:, 3 * which + 2 : 3 * which + 3]
    offset = shift - jnp.where(upper, mean[:, 0:1], mean[:, 1:2]) * gain
    value = total_ref[...].astype(F32) * gain + offset
    if which == 0:
        value = silu(value)
    out_ref[...] = jnp.broadcast_to(value.astype(BF16)[None], out_ref.shape)


def attention_kernel(at_ref, x_ref, w_ref, pairs_ref, w_out_ref, own_ref, part_ref, fresh_ref):
    mapped = nn(w_ref[...], x_ref[...])
    queries = jnp.transpose(mapped[:HEAD]).astype(BF16)
    fresh = jnp.transpose(mapped[HEAD:]).astype(BF16)
    queries = (queries.astype(F32) * HEAD ** (-0.5)).astype(BF16)
    queries = jnp.concatenate([queries, jnp.zeros((CELLS, HEAD), BF16)], axis=1)
    order = cell_order()
    fresh_ref[...] = nn(order, fresh).astype(BF16)
    chunk = 4
    highest = jnp.full((CELLS, 1), -jnp.inf, F32)
    denominator = jnp.zeros((CELLS, 1), F32)
    weighted = jnp.zeros((CELLS, 2 * HEAD), F32)
    for step in range(NS // chunk):
        blocks = []
        for k in range(chunk):
            strip = chunk * step + k
            blocks.append(jnp.where(at_ref[1] == strip, fresh, pairs_ref[strip]))
        pairs = jnp.concatenate(blocks, axis=0)
        scores = nt(queries, pairs)
        raised = jnp.maximum(highest, jnp.max(scores, axis=1, keepdims=True))
        factor = jnp.exp(highest - raised)
        weights = jnp.exp(scores - raised)
        denominator = denominator * factor + jnp.sum(weights, axis=1, keepdims=True)
        weighted = weighted * factor + nn(weights.astype(BF16), pairs)
        highest = raised
    attended = nn(order, (weighted / denominator).astype(BF16)).astype(BF16)
    own = nt(order, own_ref[...]).astype(BF16)
    pick = one_hot(iota((OC, C), 1) == iota((OC, C), 0) + at_ref[0] * OC, BF16)
    part = nt(attended, w_out_ref[...]) + nn(own, pick)
    part_ref[...] = part.astype(BF16).reshape(part_ref.shape)


def output_kernel(parts_ref, out_ref):
    total = jnp.sum(parts_ref[...].astype(F32), axis=0)
    for r in range(PC):
        out_ref[r] = total[PC * r : PC * (r + 1), :].astype(BF16)


def call(kernel, name, outs, scalars=0, mib=16):
    def run(*args):
        specs = [pl.BlockSpec(memory_space=pltpu.SMEM)] * scalars
        specs += [pl.BlockSpec(memory_space=pltpu.VMEM)] * (len(args) - scalars)
        return pl.pallas_call(
            kernel,
            out_shape=[jax.ShapeDtypeStruct(*out) for out in outs],
            in_specs=specs,
            out_specs=[pl.BlockSpec(memory_space=pltpu.VMEM)] * len(outs),
            compiler_params=pltpu.CompilerParams(vmem_limit_bytes=mib * 2**20),
            name=name,
        )(*args)

    return run


def to_every(copies, axis):
    return lax.all_to_all(copies, axis, split_axis=0, concat_axis=0, tiled=True)


def beside(value, step):
    pairs = [(i, i + step) for i in range(NS) if 0 <= i + step < NS]
    return lax.ppermute(value, PCOL, pairs)


def shards(
    latent,
    norm_scale,
    norm_shift,
    time_shift,
    conv_bias,
    conv_one,
    conv_two,
    w_qkv,
    w_out,
    stale_kv,
):
    depth, line, core = (lax.axis_index(axis) for axis in PCOL)
    at = jnp.stack([lax.axis_index(PROW), core * 16 + line * 4 + depth]).astype(jnp.int32)
    pairs = stale_kv.reshape(CELLS, 2 * HEAD)
    for axis in PCOL:
        pairs = lax.all_gather(pairs, axis, axis=0)
    pairs = pairs.reshape(NS, CELLS, 2 * HEAD)
    sums_out = ((NS, 1, 128), F32)
    every = ((NP, OC, CELLS), BF16)
    conv_out = [((OC, CELLS), F32), ((OC, LR), F32), ((OC, LR), F32)]
    (cols,) = call(columns_kernel, "columns", [((OC, 128), F32)], scalars=1)(
        at, norm_scale, norm_shift, conv_bias, time_shift.reshape(1, C)
    )

    def finish(which, mid, left, right, *more):
        kind = (F32, BF16)[which]
        total, sums = call(
            functools.partial(finish_kernel, which),
            f"finish{which}",
            [((OC, CELLS), kind), sums_out],
        )(mid, beside(right, 1), beside(left, -1), cols, *more)
        (copies,) = call(functools.partial(norm_kernel, which), f"norm{which}", [every])(
            total, to_every(sums, PCOL), cols
        )
        return total, to_every(copies, PROW).reshape(C, CELLS)

    (block,) = call(pack_kernel, "pack", [((NP, BLOCK, 128), BF16)])(latent, w_out)
    block = to_every(block, PROW)
    (sums,) = call(stats_cells_kernel, "stats", [sums_out])(block)
    sums = to_every(sums, PCOL)
    (w_part,) = call(unpack_kernel, "unpack", [((C, 128), BF16)])(block)
    mid, left, right, own = call(
        conv_cells_kernel, "conv1", conv_out + [((OC, CELLS), F32)], scalars=1
    )(at, block, sums, norm_scale, norm_shift, conv_one.reshape(9 * OC, C))
    _, field = finish(0, mid, left, right)
    mid, left, right = call(conv_channels_kernel, "conv2", conv_out)(
        field, conv_two.reshape(9 * OC, C)
    )
    resnet, field = finish(1, mid, left, right, own)
    parts, fresh = call(
        attention_kernel,
        "attention",
        [((NP, NP, C), BF16), ((CELLS, 2 * HEAD), BF16)],
        scalars=1,
        mib=32,
    )(at, field, w_qkv, pairs, w_part, resnet)
    (out,) = call(output_kernel, "output", [((PC, PC, C), BF16)])(to_every(parts, PROW))
    return out, fresh.reshape(LR, PC, 1, 2 * HEAD)


def solution(mesh):
    torus = Mesh(
        mesh.devices.reshape(2, 8, 4, 4, 2), ("prow_0", "prow_1", "pcol_0", "pcol_1", "pcol_2")
    )
    in_specs = (
        P(PROW, PCOL, None),
        P(),
        P(),
        P(),
        P(),
        P(None, None, PROW, None),
        P(None, None, PROW, None),
        P(PROW, None),
        P(PROW, None),
        P(None, PCOL, PROW, None),
    )
    out_specs = (P(PROW, PCOL, None), P(None, PCOL, PROW, None))
    return jax.shard_map(
        shards, mesh=torus, in_specs=in_specs, out_specs=out_specs, check_vma=False
    )
```

```python
import functools

import jax
import jax.numpy as jnp
from jax import lax
from jax.experimental import pallas as pl
from jax.experimental.pallas import tpu as pltpu
from jax.sharding import Mesh
from jax.sharding import PartitionSpec as P

GROUPS = 32
HEAD = 64
PROW = ("prow_0", "prow_1")
PCOL = ("pcol_0", "pcol_1", "pcol_2")
HOPS = (("pcol_0", 1), ("pcol_0", 2), ("pcol_1", 1), ("pcol_1", 2), ("pcol_2", 1))
EPSILON = 1e-05
F32 = jnp.float32
BF16 = jnp.bfloat16

C = 1280
GC = C // GROUPS
NP = 16
NS = 32
LR = 64
PC = 4
CELLS = LR * PC
OC = C // NP
POPULATION = float(LR * PC * NS * GC)


def iota(shape, dim):
    return lax.broadcasted_iota(jnp.int32, shape, dim)


def one_hot(mask, dtype):
    return jnp.where(mask, 1.0, 0.0).astype(dtype)


def nt(left, right, precision=None):
    return lax.dot_general(
        left, right, (((1,), (1,)), ((), ())), precision=precision, preferred_element_type=F32
    )


def nn(left, right, precision=None):
    return lax.dot_general(
        left, right, (((1,), (0,)), ((), ())), precision=precision, preferred_element_type=F32
    )


def strip_order():
    o = iota((CELLS, CELLS), 0)
    i = iota((CELLS, CELLS), 1)
    return one_hot((o % LR) * PC + o // LR == i, BF16)


def cell_order():
    o = iota((CELLS, CELLS), 1)
    i = iota((CELLS, CELLS), 0)
    return one_hot((o % LR) * PC + o // LR == i, BF16)


ROWS = OC // 5 * C // 128
PIECE = 48
BLOCK = ROWS + PIECE


def moments(sums_ref):
    sums = jnp.sum(sums_ref[...], axis=0)
    mean = sums / POPULATION
    square = pltpu.roll(mean, 128 - GROUPS, 1)
    return mean, lax.rsqrt(jnp.maximum(square - mean * mean, 0.0) + EPSILON)


def silu(v):
    return v / (1.0 + jnp.exp(-v))


def pack_kernel(latent_ref, w_ref, out_ref):
    rows = [latent_ref[r].astype(F32) for r in range(PC)]
    patch = jnp.concatenate(rows, axis=0).astype(BF16)
    for j in range(C // 128):
        chunk = patch[:, 128 * j : 128 * (j + 1)]
        out_ref[:, NP * j : NP * (j + 1), :] = jnp.broadcast_to(chunk[None], (NP, NP, 128))
    lane = iota((PIECE, 128), 1)
    for k in range(NP // 2):
        w = w_ref[:, 128 * k : 128 * (k + 1)].astype(F32)
        turned = pltpu.roll(w, HEAD, 1)
        blank = jnp.zeros((2 * PIECE - OC, 128), F32)

        def halves(left, right):
            low = jnp.concatenate([right[PIECE:], blank], axis=0)
            return jnp.where(lane < HEAD, left[:PIECE], low).astype(BF16)

        out_ref[2 * k, ROWS:, :] = halves(w, turned)
        out_ref[2 * k + 1, ROWS:, :] = halves(turned, w)


def unpack_kernel(block_ref, out_ref):
    lane = iota((PIECE, 128), 1)
    for p in range(NP):
        piece = block_ref[p, ROWS:, :].astype(F32)
        high = jnp.where(lane >= HEAD, pltpu.roll(piece, HEAD, 1), 0.0)
        low = jnp.where(lane >= HEAD, piece, 0.0)
        both = jnp.concatenate([high, low[: OC - PIECE]], axis=0)
        out_ref[OC * p : OC * (p + 1), :] = both.astype(BF16)


def columns_kernel(at_ref, scale_ref, shift_ref, bias_ref, time_ref, out_ref):
    pick = iota((OC, C), 1) == iota((OC, C), 0) + at_ref[0] * OC
    lane = iota((OC, 128), 1)
    total = jnp.zeros((OC, 128), F32)
    rows = [
        bias_ref[0:1, :] + time_ref[...],
        scale_ref[1:2, :],
        shift_ref[1:2, :],
        bias_ref[1:2, :],
        scale_ref[2:3, :],
        shift_ref[2:3, :],
    ]
    for k, row in enumerate(rows):
        col = jnp.sum(jnp.where(pick, row, 0.0), axis=1, keepdims=True)
        total = jnp.where(lane == k, col, total)
    out_ref[...] = total


def stats_cells_kernel(block_ref, out_ref):
    firsts, seconds = [], []
    for j in range(C // 128):
        x = block_ref[:, NP * j : NP * (j + 1), :].astype(F32).reshape(CELLS, 128)
        firsts.append(jnp.sum(x, axis=0, keepdims=True))
        seconds.append(jnp.sum(x * x, axis=0, keepdims=True))
    first = jnp.concatenate(firsts, axis=1)
    second = jnp.concatenate(seconds, axis=1)
    both = jnp.concatenate([first, second, jnp.zeros((6, C), F32)], axis=0)
    groups = one_hot(iota((C, 128), 0) // GC == iota((C, 128), 1), F32)
    reduced = nn(both, groups, lax.Precision.HIGHEST)
    row = reduced[0:1, :] + pltpu.roll(reduced, GROUPS, 1)[1:2, :]
    out_ref[...] = jnp.broadcast_to(row[None], out_ref.shape)


def conv_combine(products, mid_ref, to_left_ref, to_right_ref):
    lane = iota((OC, CELLS), 1)
    row = lane % LR

    def tap(a, b):
        at = (3 * a + b) * OC
        return products[at : at + OC, :]

    def rows_summed(b):
        above = jnp.where(row > 0, pltpu.roll(tap(0, b), 1, 1), 0.0)
        below = jnp.where(row < LR - 1, pltpu.roll(tap(2, b), CELLS - 1, 1), 0.0)
        return tap(1, b) + above + below

    before = rows_summed(0)
    after = rows_summed(2)
    to_right_ref[...] = before[:, CELLS - LR :]
    to_left_ref[...] = after[:, :LR]
    mid_ref[...] = (
        rows_summed(1)
        + jnp.where(lane >= LR, pltpu.roll(before, LR, 1), 0.0)
        + jnp.where(lane < CELLS - LR, pltpu.roll(after, CELLS - LR, 1), 0.0)
    )


def conv_cells_kernel(
    at_ref, block_ref, sums_ref, scale_ref, shift_ref, w_ref, mid_ref, left_ref, right_ref, own_ref
):
    mean, rstd = moments(sums_ref)
    both = jnp.concatenate([mean, rstd, jnp.zeros((6, 128), F32)], axis=0)
    groups = one_hot(iota((128, C), 1) // GC == iota((128, C), 0), F32)
    spread = nn(both, groups, lax.Precision.HIGHEST)
    gain = spread[1:2, :] * scale_ref[0:1, :]
    offset = shift_ref[0:1, :] - spread[0:1, :] * gain
    chunks = [
        block_ref[:, NP * j : NP * (j + 1), :].reshape(CELLS, 128) for j in range(C // 128)
    ]
    cells = nn(strip_order(), jnp.concatenate(chunks, axis=1))
    pick = one_hot(iota((OC, C), 1) == iota((OC, C), 0) + at_ref[0] * OC, BF16)
    own_ref[...] = nt(pick, cells.astype(BF16))
    act = silu(cells * gain + offset).astype(BF16)
    conv_combine(nt(w_ref[...], act), mid_ref, left_ref, right_ref)


def conv_channels_kernel(x_ref, w_ref, mid_ref, left_ref, right_ref):
    conv_combine(nn(w_ref[...], x_ref[...]), mid_ref, left_ref, right_ref)


def whole(x):
    return jnp.sum(jnp.sum(x, axis=0, keepdims=True), axis=1, keepdims=True)


def finish_kernel(which, mid_ref, from_left_ref, from_right_ref, cols_ref, *refs):
    total_ref, sums_ref = refs[-2:]
    sides = jnp.concatenate(
        [from_left_ref[...], jnp.zeros((OC, CELLS - 2 * LR), F32), from_right_ref[...]], axis=1
    )
    total = mid_ref[...] + sides + cols_ref[:, 3 * which : 3 * which + 1]
    if which == 1:
        total = refs[0][...] + total
        total_ref[...] = total.astype(BF16)
        total = total.astype(BF16).astype(F32)
    else:
        total_ref[...] = total
    lane = iota((1, 128), 1)
    row = jnp.zeros((1, 128), F32)
    for k in range(2):
        half = total[GC * k : GC * (k + 1)]
        row = jnp.where(lane == k, whole(half), row)
        row = jnp.where(lane == k + GROUPS, whole(half * half), row)
    sums_ref[...] = jnp.broadcast_to(row[None], sums_ref.shape)


def norm_kernel(which, total_ref, sums_ref, cols_ref, out_ref):
    mean, rstd = moments(sums_ref)
    upper = iota((OC, 1), 0) < GC
    gain = jnp.where(upper, rstd[:, 0:1], rstd[:, 1:2]) * cols_ref[:, 3 * which + 1 : 3 * which + 2]
    shift = cols_ref[:, 3 * which + 2 : 3 * which + 3]
    offset = shift - jnp.where(upper, mean[:, 0:1], mean[:, 1:2]) * gain
    value = total_ref[...].astype(F32) * gain + offset
    if which == 0:
        value = silu(value)
    out_ref[...] = jnp.broadcast_to(value.astype(BF16)[None], out_ref.shape)


def join_kernel(left_ref, right_ref, out_ref):
    count = left_ref.shape[0]
    out_ref[:count] = left_ref[...]
    out_ref[count:] = right_ref[...]


def attention_kernel(
    at_ref, x_ref, w_ref, near_ref, far_ref, w_out_ref, own_ref, part_ref, fresh_ref
):
    mapped = nn(w_ref[...], x_ref[...])
    queries = jnp.transpose(mapped[:HEAD]).astype(BF16)
    fresh = jnp.transpose(mapped[HEAD:]).astype(BF16)
    queries = (queries.astype(F32) * HEAD ** (-0.5)).astype(BF16)
    queries = jnp.concatenate([queries, jnp.zeros((CELLS, HEAD), BF16)], axis=1)
    order = cell_order()
    fresh_ref[...] = nn(order, fresh).astype(BF16)
    chunk = 4
    highest = jnp.full((CELLS, 1), -jnp.inf, F32)
    denominator = jnp.zeros((CELLS, 1), F32)
    weighted = jnp.zeros((CELLS, 2 * HEAD), F32)
    for step in range(NS // chunk):
        half = (near_ref, far_ref)[step // (NS // chunk // 2)]
        start = chunk * step % (NS // 2)
        pairs = half[start : start + chunk].reshape(chunk * CELLS, 2 * HEAD)
        if step == 0:
            pairs = jnp.concatenate([fresh, pairs[CELLS:]], axis=0)
        scores = nt(queries, pairs)
        raised = jnp.maximum(highest, jnp.max(scores, axis=1, keepdims=True))
        factor = jnp.exp(highest - raised)
        weights = jnp.exp(scores - raised)
        denominator = denominator * factor + jnp.sum(weights, axis=1, keepdims=True)
        weighted = weighted * factor + nn(weights.astype(BF16), pairs)
        highest = raised
    attended = nn(order, (weighted / denominator).astype(BF16)).astype(BF16)
    own = nt(order, own_ref[...]).astype(BF16)
    pick = one_hot(iota((OC, C), 1) == iota((OC, C), 0) + at_ref[0] * OC, BF16)
    part = nt(attended, w_out_ref[...]) + nn(own, pick)
    part_ref[...] = part.astype(BF16).reshape(part_ref.shape)


def output_kernel(parts_ref, out_ref):
    total = jnp.sum(parts_ref[...].astype(F32), axis=0)
    for r in range(PC):
        out_ref[r] = total[PC * r : PC * (r + 1), :].astype(BF16)


def call(kernel, outs, scalars=0, mib=8):
    def run(*args):
        specs = [pl.BlockSpec(memory_space=pltpu.SMEM)] * scalars
        specs += [pl.BlockSpec(memory_space=pltpu.VMEM)] * (len(args) - scalars)
        return pl.pallas_call(
            kernel,
            out_shape=[jax.ShapeDtypeStruct(*out) for out in outs],
            in_specs=specs,
            out_specs=[pl.BlockSpec(memory_space=pltpu.VMEM)] * len(outs),
            compiler_params=pltpu.CompilerParams(vmem_limit_bytes=mib * 2**20),
        )(*args)

    return run


def to_every(copies, axis):
    return lax.all_to_all(copies, axis, split_axis=0, concat_axis=0, tiled=True)


def beside(value, step):
    pairs = [(i, i + step) for i in range(NS) if 0 <= i + step < NS]
    return lax.ppermute(value, PCOL, pairs)


def shards(
    latent,
    norm_scale,
    norm_shift,
    time_shift,
    conv_bias,
    conv_one,
    conv_two,
    w_qkv,
    w_out,
    stale_kv,
):
    at = lax.axis_index(PROW).astype(jnp.int32).reshape(1)
    near = stale_kv.reshape(1, CELLS, 2 * HEAD)
    for step, (axis, bit) in enumerate(HOPS):
        count = lax.axis_size(axis)
        far = lax.ppermute(near, axis, [(i, i ^ bit) for i in range(count)])
        if step < len(HOPS) - 1:
            out = ((2 * near.shape[0], CELLS, 2 * HEAD), BF16)
            (near,) = call(join_kernel, [out])(near, far)
    sums_out = ((NS, 1, 128), F32)
    every = ((NP, OC, CELLS), BF16)
    conv_out = [((OC, CELLS), F32), ((OC, LR), F32), ((OC, LR), F32)]
    (cols,) = call(columns_kernel, [((OC, 128), F32)], scalars=1)(
        at, norm_scale, norm_shift, conv_bias, time_shift.reshape(1, C)
    )

    def finish(which, mid, left, right, *more):
        kind = (F32, BF16)[which]
        total, sums = call(
            functools.partial(finish_kernel, which), [((OC, CELLS), kind), sums_out]
        )(mid, beside(right, 1), beside(left, -1), cols, *more)
        (copies,) = call(functools.partial(norm_kernel, which), [every])(
            total, to_every(sums, PCOL), cols
        )
        return total, to_every(copies, PROW).reshape(C, CELLS)

    (block,) = call(pack_kernel, [((NP, BLOCK, 128), BF16)])(latent, w_out)
    block = to_every(block, PROW)
    (sums,) = call(stats_cells_kernel, [sums_out])(block)
    sums = to_every(sums, PCOL)
    (w_part,) = call(unpack_kernel, [((C, 128), BF16)])(block)
    mid, left, right, own = call(
        conv_cells_kernel, conv_out + [((OC, CELLS), F32)], scalars=1
    )(at, block, sums, norm_scale, norm_shift, conv_one.reshape(9 * OC, C))
    _, field = finish(0, mid, left, right)
    mid, left, right = call(conv_channels_kernel, conv_out)(field, conv_two.reshape(9 * OC, C))
    resnet, field = finish(1, mid, left, right, own)
    parts, fresh = call(
        attention_kernel, [((NP, NP, C), BF16), ((CELLS, 2 * HEAD), BF16)], scalars=1, mib=16
    )(at, field, w_qkv, near, far, w_part, resnet)
    (out,) = call(output_kernel, [((PC, PC, C), BF16)])(to_every(parts, PROW))
    return out, fresh.reshape(LR, PC, 1, 2 * HEAD)


def solution(mesh):
    torus = Mesh(
        mesh.devices.reshape(2, 8, 4, 4, 2), ("prow_0", "prow_1", "pcol_0", "pcol_1", "pcol_2")
    )
    in_specs = (
        P(PROW, PCOL, None),
        P(),
        P(),
        P(),
        P(),
        P(None, None, PROW, None),
        P(None, None, PROW, None),
        P(PROW, None),
        P(PROW, None),
        P(None, PCOL, PROW, None),
    )
    out_specs = (P(PROW, PCOL, None), P(None, PCOL, PROW, None))

    return jax.shard_map(
        shards, mesh=torus, in_specs=in_specs, out_specs=out_specs, check_vma=False
    )
```

```python
import functools

import jax
import jax.numpy as jnp
from jax import lax
from jax.experimental import pallas as pl
from jax.experimental.pallas import tpu as pltpu
from jax.sharding import Mesh
from jax.sharding import PartitionSpec as P

GROUPS = 32
HEAD = 64
PROW = ("prow_0", "prow_1")
PCOL = ("pcol_0", "pcol_1", "pcol_2")
HOPS = (("pcol_0", 1), ("pcol_0", 2), ("pcol_1", 1), ("pcol_1", 2), ("pcol_2", 1))
EPSILON = 1e-05
F32 = jnp.float32
BF16 = jnp.bfloat16

C = 1280
GC = C // GROUPS
NP = 16
NS = 32
LR = 64
PC = 4
CELLS = LR * PC
OC = C // NP
POPULATION = float(LR * PC * NS * GC)


def iota(shape, dim):
    return lax.broadcasted_iota(jnp.int32, shape, dim)


def one_hot(mask, dtype):
    return jnp.where(mask, 1.0, 0.0).astype(dtype)


def nt(left, right, precision=None):
    return lax.dot_general(
        left, right, (((1,), (1,)), ((), ())), precision=precision, preferred_element_type=F32
    )


def nn(left, right, precision=None):
    return lax.dot_general(
        left, right, (((1,), (0,)), ((), ())), precision=precision, preferred_element_type=F32
    )


def strip_order():
    o = iota((CELLS, CELLS), 0)
    i = iota((CELLS, CELLS), 1)
    return one_hot((o % LR) * PC + o // LR == i, BF16)


def cell_order():
    o = iota((CELLS, CELLS), 1)
    i = iota((CELLS, CELLS), 0)
    return one_hot((o % LR) * PC + o // LR == i, BF16)


ROWS = OC // 5 * C // 128
PIECE = 48
BLOCK = ROWS + PIECE


def moments(sums_ref):
    sums = jnp.sum(sums_ref[...], axis=0)
    mean = sums / POPULATION
    square = pltpu.roll(mean, 128 - GROUPS, 1)
    return mean, lax.rsqrt(jnp.maximum(square - mean * mean, 0.0) + EPSILON)


def silu(v):
    return v / (1.0 + jnp.exp(-v))


def pack_kernel(latent_hbm, w_hbm, out_ref, latent_ref, w_ref, sems):
    copies = [
        pltpu.make_async_copy(latent_hbm, latent_ref, sems.at[0]),
        pltpu.make_async_copy(w_hbm, w_ref, sems.at[1]),
    ]
    for copy in copies:
        copy.start()
    copies[0].wait()
    rows = [latent_ref[r].astype(F32) for r in range(PC)]
    patch = jnp.concatenate(rows, axis=0).astype(BF16)
    for j in range(C // 128):
        chunk = patch[:, 128 * j : 128 * (j + 1)]
        out_ref[:, NP * j : NP * (j + 1), :] = jnp.broadcast_to(chunk[None], (NP, NP, 128))
    copies[1].wait()
    lane = iota((PIECE, 128), 1)
    for k in range(NP // 2):
        w = w_ref[:, 128 * k : 128 * (k + 1)].astype(F32)
        turned = pltpu.roll(w, HEAD, 1)
        blank = jnp.zeros((2 * PIECE - OC, 128), F32)

        def halves(left, right):
            low = jnp.concatenate([right[PIECE:], blank], axis=0)
            return jnp.where(lane < HEAD, left[:PIECE], low).astype(BF16)

        out_ref[2 * k, ROWS:, :] = halves(w, turned)
        out_ref[2 * k + 1, ROWS:, :] = halves(turned, w)


def unpack_kernel(block_ref, out_ref):
    lane = iota((PIECE, 128), 1)
    for p in range(NP):
        piece = block_ref[p, ROWS:, :].astype(F32)
        high = jnp.where(lane >= HEAD, pltpu.roll(piece, HEAD, 1), 0.0)
        low = jnp.where(lane >= HEAD, piece, 0.0)
        both = jnp.concatenate([high, low[: OC - PIECE]], axis=0)
        out_ref[OC * p : OC * (p + 1), :] = both.astype(BF16)


def columns_kernel(at_ref, scale_ref, shift_ref, bias_ref, time_ref, out_ref):
    pick = iota((OC, C), 1) == iota((OC, C), 0) + at_ref[0] * OC
    lane = iota((OC, 128), 1)
    total = jnp.zeros((OC, 128), F32)
    rows = [
        bias_ref[0:1, :] + time_ref[...],
        scale_ref[1:2, :],
        shift_ref[1:2, :],
        bias_ref[1:2, :],
        scale_ref[2:3, :],
        shift_ref[2:3, :],
    ]
    for k, row in enumerate(rows):
        col = jnp.sum(jnp.where(pick, row, 0.0), axis=1, keepdims=True)
        total = jnp.where(lane == k, col, total)
    out_ref[...] = total


def strip_chunk(block_ref, j):
    return block_ref[:, NP * j : NP * (j + 1), :].reshape(CELLS, 128)


def stats_cells_kernel(block_ref, out_ref, leftmost_ref, rightmost_ref):
    firsts, seconds = [], []
    row = iota((2 * LR, CELLS), 0)
    wanted = jnp.where(row < LR, row * PC, (row - LR) * PC + PC - 1)
    pick = one_hot(iota((2 * LR, CELLS), 1) == wanted, BF16)
    for j in range(C // 128):
        x = strip_chunk(block_ref, j)
        edges = nn(pick, x).astype(BF16)
        leftmost_ref[:, 128 * j : 128 * (j + 1)] = edges[:LR]
        rightmost_ref[:, 128 * j : 128 * (j + 1)] = edges[LR:]
        x = x.astype(F32)
        firsts.append(jnp.sum(x, axis=0, keepdims=True))
        seconds.append(jnp.sum(x * x, axis=0, keepdims=True))
    first = jnp.concatenate(firsts, axis=1)
    second = jnp.concatenate(seconds, axis=1)
    both = jnp.concatenate([first, second, jnp.zeros((6, C), F32)], axis=0)
    groups = one_hot(iota((C, 128), 0) // GC == iota((C, 128), 1), F32)
    reduced = nn(both, groups, lax.Precision.HIGHEST)
    row = reduced[0:1, :] + pltpu.roll(reduced, GROUPS, 1)[1:2, :]
    out_ref[...] = jnp.broadcast_to(row[None], out_ref.shape)


def tap_sums(products, b):
    row = iota((OC, products.shape[1]), 1) % LR
    above, here, below = (
        products[(3 * a + b) * OC : (3 * a + b + 1) * OC, :] for a in range(3)
    )
    above = jnp.where(row > 0, pltpu.roll(above, 1, 1), 0.0)
    below = jnp.where(row < LR - 1, pltpu.roll(below, products.shape[1] - 1, 1), 0.0)
    return here + above + below


def tap_columns(products):
    lane = iota((OC, CELLS), 1)
    before = tap_sums(products, 0)
    after = tap_sums(products, 2)
    mid = (
        tap_sums(products, 1)
        + jnp.where(lane >= LR, pltpu.roll(before, LR, 1), 0.0)
        + jnp.where(lane < CELLS - LR, pltpu.roll(after, CELLS - LR, 1), 0.0)
    )
    return before, mid, after


def with_sides(mid, left, right):
    blank = jnp.zeros((OC, CELLS - 2 * LR), F32)
    return mid + jnp.concatenate([left, blank, right], axis=1)


def conv_cells_kernel(
    at_ref,
    block_ref,
    sums_ref,
    scale_ref,
    shift_ref,
    w_ref,
    left_ref,
    right_ref,
    cols_ref,
    total_ref,
    out_sums_ref,
    own_ref,
):
    mean, rstd = moments(sums_ref)
    both = jnp.concatenate([mean, rstd, jnp.zeros((6, 128), F32)], axis=0)
    groups = one_hot(iota((128, C), 1) // GC == iota((128, C), 0), F32)
    spread = nn(both, groups, lax.Precision.HIGHEST)
    gain = spread[1:2, :] * scale_ref[0:1, :]
    offset = shift_ref[0:1, :] - spread[0:1, :] * gain
    chunks = [strip_chunk(block_ref, j) for j in range(C // 128)]
    cells = nn(strip_order(), jnp.concatenate(chunks, axis=1))
    pick = one_hot(iota((OC, C), 1) == iota((OC, C), 0) + at_ref[0] * OC, BF16)
    own_ref[...] = nt(pick, cells.astype(BF16))
    _, mid, _ = tap_columns(nt(w_ref[...], silu(cells * gain + offset).astype(BF16)))
    sides = jnp.concatenate([left_ref[...], right_ref[...]], axis=0).astype(F32)
    sides = silu(sides * gain + offset)
    row = iota((2 * LR, 1), 0)
    first = jnp.where(at_ref[1] > 0, 0, LR)
    last = jnp.where(at_ref[1] < NS - 1, 2 * LR, LR)
    sides = jnp.where((row >= first) & (row < last), sides, 0.0).astype(BF16)
    products = nt(w_ref[...], sides)
    left = tap_sums(products, 0)[:, :LR]
    right = tap_sums(products, 2)[:, LR:]
    total = with_sides(mid, left, right) + cols_ref[:, 0:1]
    total_ref[...] = total
    own_sums(total, out_sums_ref)


def conv_channels_kernel(x_ref, w_ref, mid_ref, to_left_ref, to_right_ref):
    before, mid, after = tap_columns(nn(w_ref[...], x_ref[...]))
    to_right_ref[...] = before[:, CELLS - LR :]
    to_left_ref[...] = after[:, :LR]
    mid_ref[...] = mid


def whole(x):
    return jnp.sum(jnp.sum(x, axis=0, keepdims=True), axis=1, keepdims=True)


def own_sums(total, sums_ref):
    lane = iota((1, 128), 1)
    row = jnp.zeros((1, 128), F32)
    for k in range(2):
        half = total[GC * k : GC * (k + 1)]
        row = jnp.where(lane == k, whole(half), row)
        row = jnp.where(lane == k + GROUPS, whole(half * half), row)
    sums_ref[...] = jnp.broadcast_to(row[None], sums_ref.shape)


def finish_kernel(mid_ref, from_left_ref, from_right_ref, cols_ref, own_ref, total_ref, sums_ref):
    total = with_sides(mid_ref[...], from_left_ref[...], from_right_ref[...])
    total = (own_ref[...] + total + cols_ref[:, 3:4]).astype(BF16)
    total_ref[...] = total
    own_sums(total.astype(F32), sums_ref)


def norm_kernel(which, total_ref, sums_ref, cols_ref, out_ref):
    mean, rstd = moments(sums_ref)
    upper = iota((OC, 1), 0) < GC
    gain = jnp.where(upper, rstd[:, 0:1], rstd[:, 1:2]) * cols_ref[:, 3 * which + 1 : 3 * which + 2]
    shift = cols_ref[:, 3 * which + 2 : 3 * which + 3]
    offset = shift - jnp.where(upper, mean[:, 0:1], mean[:, 1:2]) * gain
    value = total_ref[...].astype(F32) * gain + offset
    if which == 0:
        value = silu(value)
    out_ref[...] = jnp.broadcast_to(value.astype(BF16)[None], out_ref.shape)


def join_kernel(left_ref, right_ref, out_ref, sems):
    count = left_ref.shape[0]
    copies = [
        pltpu.make_async_copy(left_ref, out_ref.at[pl.ds(0, count)], sems.at[0]),
        pltpu.make_async_copy(right_ref, out_ref.at[pl.ds(count, count)], sems.at[1]),
    ]
    for copy in copies:
        copy.start()
    for copy in copies:
        copy.wait()


def attention_kernel(
    at_ref,
    x_ref,
    w_ref,
    w_out_ref,
    own_ref,
    near_ref,
    far_ref,
    part_ref,
    fresh_ref,
    held_ref,
    sems,
):
    copies = [
        pltpu.make_async_copy(half, held_ref.at[k], sems.at[k])
        for k, half in enumerate((near_ref, far_ref))
    ]
    for copy in copies:
        copy.start()
    mapped = nn(w_ref[...], x_ref[...])
    queries = jnp.transpose(mapped[:HEAD]).astype(BF16)
    fresh = jnp.transpose(mapped[HEAD:]).astype(BF16)
    queries = (queries.astype(F32) * HEAD ** (-0.5)).astype(BF16)
    queries = jnp.concatenate([queries, jnp.zeros((CELLS, HEAD), BF16)], axis=1)
    order = cell_order()
    fresh_ref[...] = nn(order, fresh).astype(BF16)
    chunk = 4
    highest = jnp.full((CELLS, 1), -jnp.inf, F32)
    denominator = jnp.zeros((CELLS, 1), F32)
    weighted = jnp.zeros((CELLS, 2 * HEAD), F32)
    for step in range(NS // chunk):
        half, start = divmod(chunk * step, NS // 2)
        if start == 0:
            copies[half].wait()
        pairs = held_ref[half, start : start + chunk].reshape(chunk * CELLS, 2 * HEAD)
        if step == 0:
            pairs = jnp.concatenate([fresh, pairs[CELLS:]], axis=0)
        scores = nt(queries, pairs)
        raised = jnp.maximum(highest, jnp.max(scores, axis=1, keepdims=True))
        factor = jnp.exp(highest - raised)
        weights = jnp.exp(scores - raised)
        denominator = denominator * factor + jnp.sum(weights, axis=1, keepdims=True)
        weighted = weighted * factor + nn(weights.astype(BF16), pairs)
        highest = raised
    attended = nn(order, (weighted / denominator).astype(BF16)).astype(BF16)
    own = nt(order, own_ref[...]).astype(BF16)
    pick = one_hot(iota((OC, C), 1) == iota((OC, C), 0) + at_ref[0] * OC, BF16)
    part = nt(attended, w_out_ref[...]) + nn(own, pick)
    part_ref[...] = part.astype(BF16).reshape(part_ref.shape)


def output_kernel(parts_ref, out_ref):
    total = jnp.sum(parts_ref[...].astype(F32), axis=0)
    for r in range(PC):
        out_ref[r] = total[PC * r : PC * (r + 1), :].astype(BF16)


def call(kernel, outs, scalars=0, outer=0, mib=8, space=pltpu.VMEM, scratch=()):
    def run(*args):
        args = list(args)
        for k in range(len(args) - outer, len(args)):
            args[k] = pltpu.with_memory_space_constraint(args[k], pltpu.HBM)
        specs = [pl.BlockSpec(memory_space=pltpu.SMEM)] * scalars
        specs += [pl.BlockSpec(memory_space=pltpu.VMEM)] * (len(args) - scalars - outer)
        specs += [pl.BlockSpec(memory_space=pltpu.HBM)] * outer
        return pl.pallas_call(
            kernel,
            out_shape=[
                pltpu.HBM(*out) if space is pltpu.HBM else jax.ShapeDtypeStruct(*out) for out in outs
            ],
            in_specs=specs,
            out_specs=[pl.BlockSpec(memory_space=space)] * len(outs),
            scratch_shapes=list(scratch),
            compiler_params=pltpu.CompilerParams(vmem_limit_bytes=mib * 2**20),
        )(*args)

    return run


def to_every(copies, axis):
    return lax.all_to_all(copies, axis, split_axis=0, concat_axis=0, tiled=True)


def beside(value, step):
    pairs = [(i, i + step) for i in range(NS) if 0 <= i + step < NS]
    return lax.ppermute(value, PCOL, pairs)


def shards(
    latent,
    norm_scale,
    norm_shift,
    time_shift,
    conv_bias,
    conv_one,
    conv_two,
    w_qkv,
    w_out,
    stale_kv,
):
    at = jnp.stack([lax.axis_index(PROW), lax.axis_index(PCOL)]).astype(jnp.int32)
    near = stale_kv.reshape(1, CELLS, 2 * HEAD)
    for step, (axis, bit) in enumerate(HOPS):
        count = lax.axis_size(axis)
        far = lax.ppermute(near, axis, [(i, i ^ bit) for i in range(count)])
        if step < len(HOPS) - 1:
            out = ((2 * near.shape[0], CELLS, 2 * HEAD), BF16)
            (near,) = call(
                join_kernel,
                [out],
                outer=2,
                space=pltpu.HBM,
                scratch=[pltpu.SemaphoreType.DMA((2,))],
            )(near, far)
    sums_out = ((NS, 1, 128), F32)
    every = ((NP, OC, CELLS), BF16)
    tile = ((OC, CELLS), F32)
    edge = ((LR, C), BF16)
    (cols,) = call(columns_kernel, [((OC, 128), F32)], scalars=1)(
        at, norm_scale, norm_shift, conv_bias, time_shift.reshape(1, C)
    )

    def gathered(which, total, sums):
        sums = to_every(sums, PCOL)
        (copies,) = call(functools.partial(norm_kernel, which), [every])(total, sums, cols)
        return to_every(copies, PROW).reshape(C, CELLS)

    (block,) = call(
        pack_kernel,
        [((NP, BLOCK, 128), BF16)],
        outer=2,
        scratch=[
            pltpu.VMEM((PC, PC, C), BF16),
            pltpu.VMEM(w_out.shape, BF16),
            pltpu.SemaphoreType.DMA((2,)),
        ],
    )(latent, w_out)
    block = to_every(block, PROW)
    sums, leftmost, rightmost = call(stats_cells_kernel, [sums_out, edge, edge])(block)
    sums = to_every(sums, PCOL)
    left, right = beside(rightmost, 1), beside(leftmost, -1)
    (w_part,) = call(unpack_kernel, [((C, 128), BF16)])(block)
    total, sums, own = call(conv_cells_kernel, [tile, sums_out, tile], scalars=1)(
        at,
        block,
        sums,
        norm_scale,
        norm_shift,
        conv_one.reshape(9 * OC, C),
        left,
        right,
        cols,
    )
    field = gathered(0, total, sums)
    mid, left, right = call(
        conv_channels_kernel, [tile, ((OC, LR), F32), ((OC, LR), F32)]
    )(field, conv_two.reshape(9 * OC, C))
    left, right = beside(right, 1), beside(left, -1)
    resnet, sums = call(finish_kernel, [((OC, CELLS), BF16), sums_out])(mid, left, right, cols, own)
    field = gathered(1, resnet, sums)
    parts, fresh = call(
        attention_kernel,
        [((NP, NP, C), BF16), ((CELLS, 2 * HEAD), BF16)],
        scalars=1,
        outer=2,
        mib=16,
        scratch=[
            pltpu.VMEM((2, NS // 2, CELLS, 2 * HEAD), BF16),
            pltpu.SemaphoreType.DMA((2,)),
        ],
    )(at, field, w_qkv, w_part, resnet, near, far)
    (out,) = call(output_kernel, [((PC, PC, C), BF16)])(to_every(parts, PROW))
    return out, fresh.reshape(LR, PC, 1, 2 * HEAD)


def solution(mesh):
    torus = Mesh(
        mesh.devices.reshape(2, 8, 4, 4, 2), ("prow_0", "prow_1", "pcol_0", "pcol_1", "pcol_2")
    )
    in_specs = (
        P(PROW, PCOL, None),
        P(),
        P(),
        P(),
        P(),
        P(None, None, PROW, None),
        P(None, None, PROW, None),
        P(PROW, None),
        P(PROW, None),
        P(None, PCOL, PROW, None),
    )
    out_specs = (P(PROW, PCOL, None), P(None, PCOL, PROW, None))

    return jax.shard_map(
        shards, mesh=torus, in_specs=in_specs, out_specs=out_specs, check_vma=False
    )
```

```python
import functools

import jax
import jax.numpy as jnp
from jax import lax
from jax.experimental import pallas as pl
from jax.experimental.pallas import tpu as pltpu
from jax.sharding import Mesh
from jax.sharding import PartitionSpec as P

GROUPS = 32
HEAD = 64
PROW = ("prow_0", "prow_1")
PCOL = ("pcol_0", "pcol_1", "pcol_2")
HOPS = (("pcol_0", 1), ("pcol_0", 2), ("pcol_1", 1), ("pcol_1", 2), ("pcol_2", 1))
EPSILON = 1e-05
F32 = jnp.float32
BF16 = jnp.bfloat16

C = 1280
GC = C // GROUPS
NP = 16
NS = 32
LR = 64
PC = 4
CELLS = LR * PC
OC = C // NP
POPULATION = float(LR * PC * NS * GC)


def iota(shape, dim):
    return lax.broadcasted_iota(jnp.int32, shape, dim)


def one_hot(mask, dtype):
    return jnp.where(mask, 1.0, 0.0).astype(dtype)


def nt(left, right, precision=None):
    return lax.dot_general(
        left, right, (((1,), (1,)), ((), ())), precision=precision, preferred_element_type=F32
    )


def nn(left, right, precision=None):
    return lax.dot_general(
        left, right, (((1,), (0,)), ((), ())), precision=precision, preferred_element_type=F32
    )


def strip_order():
    o = iota((CELLS, CELLS), 0)
    i = iota((CELLS, CELLS), 1)
    return one_hot((o % LR) * PC + o // LR == i, BF16)


def cell_order():
    o = iota((CELLS, CELLS), 1)
    i = iota((CELLS, CELLS), 0)
    return one_hot((o % LR) * PC + o // LR == i, BF16)


ROWS = OC // 5 * C // 128
PIECE = 48
BLOCK = ROWS + PIECE


def moments(sums_ref):
    sums = jnp.sum(sums_ref[...], axis=0)
    mean = sums / POPULATION
    square = pltpu.roll(mean, 128 - GROUPS, 1)
    return mean, lax.rsqrt(jnp.maximum(square - mean * mean, 0.0) + EPSILON)


def silu(v):
    return v / (1.0 + jnp.exp(-v))


def pack_kernel(latent_hbm, w_hbm, out_ref, latent_ref, w_ref, sems):
    copies = [
        pltpu.make_async_copy(latent_hbm, latent_ref, sems.at[0]),
        pltpu.make_async_copy(w_hbm, w_ref, sems.at[1]),
    ]
    for copy in copies:
        copy.start()
    copies[0].wait()
    rows = [latent_ref[r].astype(F32) for r in range(PC)]
    patch = jnp.concatenate(rows, axis=0).astype(BF16)
    for j in range(C // 128):
        chunk = patch[:, 128 * j : 128 * (j + 1)]
        out_ref[:, NP * j : NP * (j + 1), :] = jnp.broadcast_to(chunk[None], (NP, NP, 128))
    copies[1].wait()
    lane = iota((PIECE, 128), 1)
    for k in range(NP // 2):
        w = w_ref[:, 128 * k : 128 * (k + 1)].astype(F32)
        turned = pltpu.roll(w, HEAD, 1)
        blank = jnp.zeros((2 * PIECE - OC, 128), F32)

        def halves(left, right):
            low = jnp.concatenate([right[PIECE:], blank], axis=0)
            return jnp.where(lane < HEAD, left[:PIECE], low).astype(BF16)

        out_ref[2 * k, ROWS:, :] = halves(w, turned)
        out_ref[2 * k + 1, ROWS:, :] = halves(turned, w)


def unpack_kernel(block_ref, out_ref):
    lane = iota((PIECE, 128), 1)
    for p in range(NP):
        piece = block_ref[p, ROWS:, :].astype(F32)
        high = jnp.where(lane >= HEAD, pltpu.roll(piece, HEAD, 1), 0.0)
        low = jnp.where(lane >= HEAD, piece, 0.0)
        both = jnp.concatenate([high, low[: OC - PIECE]], axis=0)
        out_ref[OC * p : OC * (p + 1), :] = both.astype(BF16)


def columns_kernel(at_ref, scale_ref, shift_ref, bias_ref, time_ref, out_ref):
    pick = iota((OC, C), 1) == iota((OC, C), 0) + at_ref[0] * OC
    lane = iota((OC, 128), 1)
    total = jnp.zeros((OC, 128), F32)
    rows = [
        bias_ref[0:1, :] + time_ref[...],
        scale_ref[1:2, :],
        shift_ref[1:2, :],
        bias_ref[1:2, :],
        scale_ref[2:3, :],
        shift_ref[2:3, :],
    ]
    for k, row in enumerate(rows):
        col = jnp.sum(jnp.where(pick, row, 0.0), axis=1, keepdims=True)
        total = jnp.where(lane == k, col, total)
    out_ref[...] = total


def strip_chunk(block_ref, j):
    return block_ref[:, NP * j : NP * (j + 1), :].reshape(CELLS, 128)


def stats_cells_kernel(block_ref, out_ref, leftmost_ref, rightmost_ref):
    firsts, seconds = [], []
    row = iota((2 * LR, CELLS), 0)
    wanted = jnp.where(row < LR, row * PC, (row - LR) * PC + PC - 1)
    pick = one_hot(iota((2 * LR, CELLS), 1) == wanted, BF16)
    for j in range(C // 128):
        x = strip_chunk(block_ref, j)
        edges = nn(pick, x).astype(BF16)
        leftmost_ref[:, 128 * j : 128 * (j + 1)] = edges[:LR]
        rightmost_ref[:, 128 * j : 128 * (j + 1)] = edges[LR:]
        x = x.astype(F32)
        firsts.append(jnp.sum(x, axis=0, keepdims=True))
        seconds.append(jnp.sum(x * x, axis=0, keepdims=True))
    first = jnp.concatenate(firsts, axis=1)
    second = jnp.concatenate(seconds, axis=1)
    both = jnp.concatenate([first, second, jnp.zeros((6, C), F32)], axis=0)
    groups = one_hot(iota((C, 128), 0) // GC == iota((C, 128), 1), F32)
    reduced = nn(both, groups, lax.Precision.HIGHEST)
    row = reduced[0:1, :] + pltpu.roll(reduced, GROUPS, 1)[1:2, :]
    out_ref[...] = jnp.broadcast_to(row[None], out_ref.shape)


def tap_sums(products, b):
    row = iota((OC, products.shape[1]), 1) % LR
    above, here, below = (
        products[(3 * a + b) * OC : (3 * a + b + 1) * OC, :] for a in range(3)
    )
    above = jnp.where(row > 0, pltpu.roll(above, 1, 1), 0.0)
    below = jnp.where(row < LR - 1, pltpu.roll(below, products.shape[1] - 1, 1), 0.0)
    return here + above + below


def tap_columns(products):
    lane = iota((OC, CELLS), 1)
    before = tap_sums(products, 0)
    after = tap_sums(products, 2)
    mid = (
        tap_sums(products, 1)
        + jnp.where(lane >= LR, pltpu.roll(before, LR, 1), 0.0)
        + jnp.where(lane < CELLS - LR, pltpu.roll(after, CELLS - LR, 1), 0.0)
    )
    return before, mid, after


def with_sides(mid, left, right):
    blank = jnp.zeros((OC, CELLS - 2 * LR), F32)
    return mid + jnp.concatenate([left, blank, right], axis=1)


def conv_cells_kernel(
    at_ref,
    block_ref,
    sums_ref,
    scale_ref,
    shift_ref,
    w_ref,
    left_ref,
    right_ref,
    cols_ref,
    total_ref,
    out_sums_ref,
    own_ref,
):
    mean, rstd = moments(sums_ref)
    both = jnp.concatenate([mean, rstd, jnp.zeros((6, 128), F32)], axis=0)
    groups = one_hot(iota((128, C), 1) // GC == iota((128, C), 0), F32)
    spread = nn(both, groups, lax.Precision.HIGHEST)
    gain = spread[1:2, :] * scale_ref[0:1, :]
    offset = shift_ref[0:1, :] - spread[0:1, :] * gain
    chunks = [strip_chunk(block_ref, j) for j in range(C // 128)]
    cells = nn(strip_order(), jnp.concatenate(chunks, axis=1))
    pick = one_hot(iota((OC, C), 1) == iota((OC, C), 0) + at_ref[0] * OC, BF16)
    own_ref[...] = nt(pick, cells.astype(BF16))
    _, mid, _ = tap_columns(nt(w_ref[...], silu(cells * gain + offset).astype(BF16)))
    sides = jnp.concatenate([left_ref[...], right_ref[...]], axis=0).astype(F32)
    sides = silu(sides * gain + offset)
    row = iota((2 * LR, 1), 0)
    first = jnp.where(at_ref[1] > 0, 0, LR)
    last = jnp.where(at_ref[1] < NS - 1, 2 * LR, LR)
    sides = jnp.where((row >= first) & (row < last), sides, 0.0).astype(BF16)
    products = nt(w_ref[...], sides)
    left = tap_sums(products, 0)[:, :LR]
    right = tap_sums(products, 2)[:, LR:]
    total = with_sides(mid, left, right) + cols_ref[:, 0:1]
    total_ref[...] = total
    own_sums(total, out_sums_ref)


def conv_channels_kernel(x_ref, w_ref, mid_ref, to_left_ref, to_right_ref):
    before, mid, after = tap_columns(nn(w_ref[...], x_ref[...]))
    to_right_ref[...] = before[:, CELLS - LR :]
    to_left_ref[...] = after[:, :LR]
    mid_ref[...] = mid


def whole(x):
    return jnp.sum(jnp.sum(x, axis=0, keepdims=True), axis=1, keepdims=True)


def own_sums(total, sums_ref):
    lane = iota((1, 128), 1)
    row = jnp.zeros((1, 128), F32)
    for k in range(2):
        half = total[GC * k : GC * (k + 1)]
        row = jnp.where(lane == k, whole(half), row)
        row = jnp.where(lane == k + GROUPS, whole(half * half), row)
    sums_ref[...] = jnp.broadcast_to(row[None], sums_ref.shape)


def finish_kernel(mid_ref, from_left_ref, from_right_ref, cols_ref, own_ref, total_ref, sums_ref):
    total = with_sides(mid_ref[...], from_left_ref[...], from_right_ref[...])
    total = (own_ref[...] + total + cols_ref[:, 3:4]).astype(BF16)
    total_ref[...] = total
    own_sums(total.astype(F32), sums_ref)


def norm_kernel(which, total_ref, sums_ref, cols_ref, out_ref):
    mean, rstd = moments(sums_ref)
    upper = iota((OC, 1), 0) < GC
    gain = jnp.where(upper, rstd[:, 0:1], rstd[:, 1:2]) * cols_ref[:, 3 * which + 1 : 3 * which + 2]
    shift = cols_ref[:, 3 * which + 2 : 3 * which + 3]
    offset = shift - jnp.where(upper, mean[:, 0:1], mean[:, 1:2]) * gain
    value = total_ref[...].astype(F32) * gain + offset
    if which == 0:
        value = silu(value)
    out_ref[...] = jnp.broadcast_to(value.astype(BF16)[None], out_ref.shape)


def join_kernel(left_ref, right_ref, out_ref, sems):
    count = left_ref.shape[0]
    copies = [
        pltpu.make_async_copy(left_ref, out_ref.at[pl.ds(0, count)], sems.at[0]),
        pltpu.make_async_copy(right_ref, out_ref.at[pl.ds(count, count)], sems.at[1]),
    ]
    for copy in copies:
        copy.start()
    for copy in copies:
        copy.wait()


def attention_kernel(
    at_ref,
    x_ref,
    w_ref,
    w_out_ref,
    own_ref,
    near_ref,
    far_ref,
    part_ref,
    fresh_ref,
    held_ref,
    sems,
):
    chunk = 4
    copies = []
    for step in range(NS // chunk):
        half, start = divmod(chunk * step, NS // 2)
        strips = pl.ds(start, chunk)
        source = (near_ref, far_ref)[half].at[strips]
        copies.append(
            pltpu.make_async_copy(source, held_ref.at[half, strips], sems.at[step])
        )
    for copy in copies:
        copy.start()
    mapped = nn(w_ref[...], x_ref[...])
    queries = jnp.transpose(mapped[:HEAD]).astype(BF16)
    fresh = jnp.transpose(mapped[HEAD:]).astype(BF16)
    queries = (queries.astype(F32) * HEAD ** (-0.5)).astype(BF16)
    queries = jnp.concatenate([queries, jnp.zeros((CELLS, HEAD), BF16)], axis=1)
    order = cell_order()
    fresh_ref[...] = nn(order, fresh).astype(BF16)
    highest = jnp.full((CELLS, 1), -jnp.inf, F32)
    denominator = jnp.zeros((CELLS, 1), F32)
    weighted = jnp.zeros((CELLS, 2 * HEAD), F32)
    for step in range(NS // chunk):
        half, start = divmod(chunk * step, NS // 2)
        copies[step].wait()
        pairs = held_ref[half, start : start + chunk].reshape(chunk * CELLS, 2 * HEAD)
        if step == 0:
            pairs = jnp.concatenate([fresh, pairs[CELLS:]], axis=0)
        scores = nt(queries, pairs)
        raised = jnp.maximum(highest, jnp.max(scores, axis=1, keepdims=True))
        factor = jnp.exp(highest - raised)
        weights = jnp.exp(scores - raised)
        denominator = denominator * factor + jnp.sum(weights, axis=1, keepdims=True)
        weighted = weighted * factor + nn(weights.astype(BF16), pairs)
        highest = raised
    attended = nn(order, (weighted / denominator).astype(BF16)).astype(BF16)
    own = nt(order, own_ref[...]).astype(BF16)
    pick = one_hot(iota((OC, C), 1) == iota((OC, C), 0) + at_ref[0] * OC, BF16)
    part = nt(attended, w_out_ref[...]) + nn(own, pick)
    part_ref[...] = part.astype(BF16).reshape(part_ref.shape)


def output_kernel(parts_ref, out_ref):
    total = jnp.sum(parts_ref[...].astype(F32), axis=0)
    for r in range(PC):
        out_ref[r] = total[PC * r : PC * (r + 1), :].astype(BF16)


def call(kernel, outs, scalars=0, outer=0, mib=8, space=pltpu.VMEM, scratch=()):
    def run(*args):
        args = list(args)
        for k in range(len(args) - outer, len(args)):
            args[k] = pltpu.with_memory_space_constraint(args[k], pltpu.HBM)
        specs = [pl.BlockSpec(memory_space=pltpu.SMEM)] * scalars
        specs += [pl.BlockSpec(memory_space=pltpu.VMEM)] * (len(args) - scalars - outer)
        specs += [pl.BlockSpec(memory_space=pltpu.HBM)] * outer
        return pl.pallas_call(
            kernel,
            out_shape=[
                pltpu.HBM(*out) if space is pltpu.HBM else jax.ShapeDtypeStruct(*out) for out in outs
            ],
            in_specs=specs,
            out_specs=[pl.BlockSpec(memory_space=space)] * len(outs),
            scratch_shapes=list(scratch),
            compiler_params=pltpu.CompilerParams(vmem_limit_bytes=mib * 2**20),
        )(*args)

    return run


def to_every(copies, axis):
    return lax.all_to_all(copies, axis, split_axis=0, concat_axis=0, tiled=True)


def beside(value, step):
    pairs = [(i, i + step) for i in range(NS) if 0 <= i + step < NS]
    return lax.ppermute(value, PCOL, pairs)


def shards(
    latent,
    norm_scale,
    norm_shift,
    time_shift,
    conv_bias,
    conv_one,
    conv_two,
    w_qkv,
    w_out,
    stale_kv,
):
    at = jnp.stack([lax.axis_index(PROW), lax.axis_index(PCOL)]).astype(jnp.int32)
    near = stale_kv.reshape(1, CELLS, 2 * HEAD)
    for step, (axis, bit) in enumerate(HOPS):
        count = lax.axis_size(axis)
        far = lax.ppermute(near, axis, [(i, i ^ bit) for i in range(count)])
        if step < len(HOPS) - 1:
            out = ((2 * near.shape[0], CELLS, 2 * HEAD), BF16)
            (near,) = call(
                join_kernel, [out], space=pltpu.HBM, scratch=[pltpu.SemaphoreType.DMA((2,))]
            )(near, far)
    sums_out = ((NS, 1, 128), F32)
    every = ((NP, OC, CELLS), BF16)
    tile = ((OC, CELLS), F32)
    edge = ((LR, C), BF16)
    (cols,) = call(columns_kernel, [((OC, 128), F32)], scalars=1)(
        at, norm_scale, norm_shift, conv_bias, time_shift.reshape(1, C)
    )

    def gathered(which, total, sums):
        sums = to_every(sums, PCOL)
        (copies,) = call(functools.partial(norm_kernel, which), [every])(total, sums, cols)
        return to_every(copies, PROW).reshape(C, CELLS)

    (block,) = call(
        pack_kernel,
        [((NP, BLOCK, 128), BF16)],
        outer=2,
        scratch=[
            pltpu.VMEM((PC, PC, C), BF16),
            pltpu.VMEM(w_out.shape, BF16),
            pltpu.SemaphoreType.DMA((2,)),
        ],
    )(latent, w_out)
    block = to_every(block, PROW)
    sums, leftmost, rightmost = call(stats_cells_kernel, [sums_out, edge, edge])(block)
    sums = to_every(sums, PCOL)
    left, right = beside(rightmost, 1), beside(leftmost, -1)
    (w_part,) = call(unpack_kernel, [((C, 128), BF16)])(block)
    total, sums, own = call(conv_cells_kernel, [tile, sums_out, tile], scalars=1)(
        at,
        block,
        sums,
        norm_scale,
        norm_shift,
        conv_one.reshape(9 * OC, C),
        left,
        right,
        cols,
    )
    field = gathered(0, total, sums)
    mid, left, right = call(
        conv_channels_kernel, [tile, ((OC, LR), F32), ((OC, LR), F32)]
    )(field, conv_two.reshape(9 * OC, C))
    left, right = beside(right, 1), beside(left, -1)
    resnet, sums = call(finish_kernel, [((OC, CELLS), BF16), sums_out])(mid, left, right, cols, own)
    field = gathered(1, resnet, sums)
    parts, fresh = call(
        attention_kernel,
        [((NP, NP, C), BF16), ((CELLS, 2 * HEAD), BF16)],
        scalars=1,
        outer=2,
        mib=16,
        scratch=[
            pltpu.VMEM((2, NS // 2, CELLS, 2 * HEAD), BF16),
            pltpu.SemaphoreType.DMA((NS // 4,)),
        ],
    )(at, field, w_qkv, w_part, resnet, near, far)
    (out,) = call(output_kernel, [((PC, PC, C), BF16)])(to_every(parts, PROW))
    return out, fresh.reshape(LR, PC, 1, 2 * HEAD)


def solution(mesh):
    torus = Mesh(
        mesh.devices.reshape(2, 8, 4, 4, 2), ("prow_0", "prow_1", "pcol_0", "pcol_1", "pcol_2")
    )
    in_specs = (
        P(PROW, PCOL, None),
        P(),
        P(),
        P(),
        P(),
        P(None, None, PROW, None),
        P(None, None, PROW, None),
        P(PROW, None),
        P(PROW, None),
        P(None, PCOL, PROW, None),
    )
    out_specs = (P(PROW, PCOL, None), P(None, PCOL, PROW, None))

    return jax.shard_map(
        shards, mesh=torus, in_specs=in_specs, out_specs=out_specs, check_vma=False
    )
```

```python
import functools

import jax
import jax.numpy as jnp
from jax import lax
from jax.experimental import pallas as pl
from jax.experimental.pallas import tpu as pltpu
from jax.sharding import Mesh
from jax.sharding import PartitionSpec as P

GROUPS = 32
HEAD = 64
PROW = ("prow_0", "prow_1")
PCOL = ("pcol_0", "pcol_1", "pcol_2")
HOPS = (("pcol_0", 1), ("pcol_0", 2), ("pcol_1", 1), ("pcol_1", 2), ("pcol_2", 1))
EPSILON = 1e-05
F32 = jnp.float32
BF16 = jnp.bfloat16

C = 1280
GC = C // GROUPS
NP = 16
NS = 32
LR = 64
PC = 4
CELLS = LR * PC
OC = C // NP
POPULATION = float(LR * PC * NS * GC)


def iota(shape, dim):
    return lax.broadcasted_iota(jnp.int32, shape, dim)


def one_hot(mask, dtype):
    return jnp.where(mask, 1.0, 0.0).astype(dtype)


def nt(left, right, precision=None):
    return lax.dot_general(
        left, right, (((1,), (1,)), ((), ())), precision=precision, preferred_element_type=F32
    )


def nn(left, right, precision=None):
    return lax.dot_general(
        left, right, (((1,), (0,)), ((), ())), precision=precision, preferred_element_type=F32
    )


def strip_order():
    o = iota((CELLS, CELLS), 0)
    i = iota((CELLS, CELLS), 1)
    return one_hot((o % LR) * PC + o // LR == i, BF16)


def cell_order():
    o = iota((CELLS, CELLS), 1)
    i = iota((CELLS, CELLS), 0)
    return one_hot((o % LR) * PC + o // LR == i, BF16)


ROWS = OC // 5 * C // 128
PIECE = 48
BLOCK = ROWS + PIECE


def moments(sums_ref):
    sums = jnp.sum(sums_ref[...], axis=0)
    mean = sums / POPULATION
    square = pltpu.roll(mean, 128 - GROUPS, 1)
    return mean, lax.rsqrt(jnp.maximum(square - mean * mean, 0.0) + EPSILON)


def silu(v):
    return v / (1.0 + jnp.exp(-v))


def pack_kernel(latent_hbm, w_hbm, out_ref, latent_ref, w_ref, sems):
    copies = [
        pltpu.make_async_copy(latent_hbm, latent_ref, sems.at[0]),
        pltpu.make_async_copy(w_hbm, w_ref, sems.at[1]),
    ]
    for copy in copies:
        copy.start()
    copies[0].wait()
    rows = [latent_ref[r].astype(F32) for r in range(PC)]
    patch = jnp.concatenate(rows, axis=0).astype(BF16)
    for j in range(C // 128):
        chunk = patch[:, 128 * j : 128 * (j + 1)]
        out_ref[:, NP * j : NP * (j + 1), :] = jnp.broadcast_to(chunk[None], (NP, NP, 128))
    copies[1].wait()
    lane = iota((PIECE, 128), 1)
    for k in range(NP // 2):
        w = w_ref[:, 128 * k : 128 * (k + 1)].astype(F32)
        turned = pltpu.roll(w, HEAD, 1)
        blank = jnp.zeros((2 * PIECE - OC, 128), F32)

        def halves(left, right):
            low = jnp.concatenate([right[PIECE:], blank], axis=0)
            return jnp.where(lane < HEAD, left[:PIECE], low).astype(BF16)

        out_ref[2 * k, ROWS:, :] = halves(w, turned)
        out_ref[2 * k + 1, ROWS:, :] = halves(turned, w)


def unpack_kernel(block_ref, out_hbm, out_ref, sem):
    lane = iota((PIECE, 128), 1)
    for p in range(NP):
        piece = block_ref[p, ROWS:, :].astype(F32)
        high = jnp.where(lane >= HEAD, pltpu.roll(piece, HEAD, 1), 0.0)
        low = jnp.where(lane >= HEAD, piece, 0.0)
        both = jnp.concatenate([high, low[: OC - PIECE]], axis=0)
        out_ref[OC * p : OC * (p + 1), :] = both.astype(BF16)
    copy = pltpu.make_async_copy(out_ref, out_hbm, sem)
    copy.start()
    copy.wait()


def columns_kernel(at_ref, scale_ref, shift_ref, bias_ref, time_ref, out_ref):
    pick = iota((OC, C), 1) == iota((OC, C), 0) + at_ref[0] * OC
    lane = iota((OC, 128), 1)
    total = jnp.zeros((OC, 128), F32)
    rows = [
        bias_ref[0:1, :] + time_ref[...],
        scale_ref[1:2, :],
        shift_ref[1:2, :],
        bias_ref[1:2, :],
        scale_ref[2:3, :],
        shift_ref[2:3, :],
    ]
    for k, row in enumerate(rows):
        col = jnp.sum(jnp.where(pick, row, 0.0), axis=1, keepdims=True)
        total = jnp.where(lane == k, col, total)
    out_ref[...] = total


def by_parity(at_ref, one, other):
    even = at_ref[1] % 2 == 0
    return jnp.where(even, one, other), jnp.where(even, other, one)


def strip_chunk(block_ref, j):
    return block_ref[:, NP * j : NP * (j + 1), :].reshape(CELLS, 128)


def stats_cells_kernel(at_ref, block_ref, out_ref, inner_ref, outer_ref):
    firsts, seconds = [], []
    row = iota((2 * LR, CELLS), 0)
    inner, outer = by_parity(at_ref, PC - 1, 0)
    wanted = jnp.where(row < LR, row * PC + inner, (row - LR) * PC + outer)
    pick = one_hot(iota((2 * LR, CELLS), 1) == wanted, BF16)
    for j in range(C // 128):
        x = strip_chunk(block_ref, j)
        edges = nn(pick, x).astype(BF16)
        inner_ref[:, 128 * j : 128 * (j + 1)] = edges[:LR]
        outer_ref[:, 128 * j : 128 * (j + 1)] = edges[LR:]
        x = x.astype(F32)
        firsts.append(jnp.sum(x, axis=0, keepdims=True))
        seconds.append(jnp.sum(x * x, axis=0, keepdims=True))
    first = jnp.concatenate(firsts, axis=1)
    second = jnp.concatenate(seconds, axis=1)
    both = jnp.concatenate([first, second, jnp.zeros((6, C), F32)], axis=0)
    groups = one_hot(iota((C, 128), 0) // GC == iota((C, 128), 1), F32)
    reduced = nn(both, groups, lax.Precision.HIGHEST)
    row = reduced[0:1, :] + pltpu.roll(reduced, GROUPS, 1)[1:2, :]
    out_ref[...] = jnp.broadcast_to(row[None], out_ref.shape)


def tap_sums(products, b):
    row = iota((OC, products.shape[1]), 1) % LR
    above, here, below = (
        products[(3 * a + b) * OC : (3 * a + b + 1) * OC, :] for a in range(3)
    )
    above = jnp.where(row > 0, pltpu.roll(above, 1, 1), 0.0)
    below = jnp.where(row < LR - 1, pltpu.roll(below, products.shape[1] - 1, 1), 0.0)
    return here + above + below


def tap_columns(products):
    lane = iota((OC, CELLS), 1)
    before = tap_sums(products, 0)
    after = tap_sums(products, 2)
    mid = (
        tap_sums(products, 1)
        + jnp.where(lane >= LR, pltpu.roll(before, LR, 1), 0.0)
        + jnp.where(lane < CELLS - LR, pltpu.roll(after, CELLS - LR, 1), 0.0)
    )
    return before, mid, after


def with_sides(mid, left, right):
    blank = jnp.zeros((OC, CELLS - 2 * LR), F32)
    return mid + jnp.concatenate([left, blank, right], axis=1)


def conv_cells_kernel(
    at_ref,
    block_ref,
    sums_ref,
    scale_ref,
    shift_ref,
    w_ref,
    inner_ref,
    outer_ref,
    cols_ref,
    total_ref,
    out_sums_ref,
    own_ref,
):
    mean, rstd = moments(sums_ref)
    both = jnp.concatenate([mean, rstd, jnp.zeros((6, 128), F32)], axis=0)
    groups = one_hot(iota((128, C), 1) // GC == iota((128, C), 0), F32)
    spread = nn(both, groups, lax.Precision.HIGHEST)
    gain = spread[1:2, :] * scale_ref[0:1, :]
    offset = shift_ref[0:1, :] - spread[0:1, :] * gain
    chunks = [strip_chunk(block_ref, j) for j in range(C // 128)]
    cells = nn(strip_order(), jnp.concatenate(chunks, axis=1))
    pick = one_hot(iota((OC, C), 1) == iota((OC, C), 0) + at_ref[0] * OC, BF16)
    own_ref[...] = nt(pick, cells.astype(BF16)).astype(BF16)
    _, mid, _ = tap_columns(nt(w_ref[...], silu(cells * gain + offset).astype(BF16)))
    right, left = by_parity(at_ref, inner_ref[...].astype(F32), outer_ref[...].astype(F32))
    sides = jnp.concatenate([left, right], axis=0)
    sides = silu(sides * gain + offset)
    row = iota((2 * LR, 1), 0)
    first = jnp.where(at_ref[1] > 0, 0, LR)
    last = jnp.where(at_ref[1] < NS - 1, 2 * LR, LR)
    sides = jnp.where((row >= first) & (row < last), sides, 0.0).astype(BF16)
    products = nt(w_ref[...], sides)
    left = tap_sums(products, 0)[:, :LR]
    right = tap_sums(products, 2)[:, LR:]
    total = with_sides(mid, left, right) + cols_ref[:, 0:1]
    total_ref[...] = total
    own_sums(total, out_sums_ref)


def conv_channels_kernel(at_ref, x_ref, w_ref, mid_ref, inner_ref, outer_ref):
    before, mid, after = tap_columns(nn(w_ref[...], x_ref[...]))
    inner, outer = by_parity(at_ref, before[:, CELLS - LR :], after[:, :LR])
    inner_ref[...] = inner
    outer_ref[...] = outer
    mid_ref[...] = mid


def whole(x):
    return jnp.sum(jnp.sum(x, axis=0, keepdims=True), axis=1, keepdims=True)


def own_sums(total, sums_ref):
    lane = iota((1, 128), 1)
    row = jnp.zeros((1, 128), F32)
    for k in range(2):
        half = total[GC * k : GC * (k + 1)]
        row = jnp.where(lane == k, whole(half), row)
        row = jnp.where(lane == k + GROUPS, whole(half * half), row)
    sums_ref[...] = jnp.broadcast_to(row[None], sums_ref.shape)


def finish_kernel(at_ref, mid_ref, inner_ref, outer_ref, cols_ref, own_ref, total_ref, sums_ref):
    right, left = by_parity(at_ref, inner_ref[...], outer_ref[...])
    total = with_sides(mid_ref[...], left, right)
    total = (own_ref[...].astype(F32) + total + cols_ref[:, 3:4]).astype(BF16)
    total_ref[...] = total
    own_sums(total.astype(F32), sums_ref)


def norm_kernel(which, total_ref, sums_ref, cols_ref, out_ref):
    mean, rstd = moments(sums_ref)
    upper = iota((OC, 1), 0) < GC
    gain = jnp.where(upper, rstd[:, 0:1], rstd[:, 1:2]) * cols_ref[:, 3 * which + 1 : 3 * which + 2]
    shift = cols_ref[:, 3 * which + 2 : 3 * which + 3]
    offset = shift - jnp.where(upper, mean[:, 0:1], mean[:, 1:2]) * gain
    value = total_ref[...].astype(F32) * gain + offset
    if which == 0:
        value = silu(value)
    out_ref[...] = jnp.broadcast_to(value.astype(BF16)[None], out_ref.shape)


def join_kernel(left_ref, right_ref, out_ref, sems):
    count = left_ref.shape[0]
    copies = [
        pltpu.make_async_copy(left_ref, out_ref.at[pl.ds(0, count)], sems.at[0]),
        pltpu.make_async_copy(right_ref, out_ref.at[pl.ds(count, count)], sems.at[1]),
    ]
    for copy in copies:
        copy.start()
    for copy in copies:
        copy.wait()


def attention_kernel(
    at_ref,
    x_ref,
    w_ref,
    w_out_ref,
    own_ref,
    far_ref,
    near_hbm,
    part_ref,
    fresh_ref,
    near_ref,
    sem,
):
    chunk = 4
    copy = pltpu.make_async_copy(near_hbm, near_ref, sem)
    copy.start()
    mapped = nn(w_ref[...], x_ref[...])
    queries = jnp.transpose(mapped[:HEAD]).astype(BF16)
    fresh = jnp.transpose(mapped[HEAD:]).astype(BF16)
    queries = (queries.astype(F32) * HEAD ** (-0.5)).astype(BF16)
    queries = jnp.concatenate([queries, jnp.zeros((CELLS, HEAD), BF16)], axis=1)
    order = cell_order()
    fresh_ref[...] = nn(order, fresh).astype(BF16)
    highest = jnp.full((CELLS, 1), -jnp.inf, F32)
    denominator = jnp.zeros((CELLS, 1), F32)
    weighted = jnp.zeros((CELLS, 2 * HEAD), F32)
    for step in range(NS // chunk):
        half, start = divmod(chunk * step, NS // 2)
        if half == 1 and start == 0:
            copy.wait()
        pairs = (far_ref, near_ref)[half][start : start + chunk]
        pairs = pairs.reshape(chunk * CELLS, 2 * HEAD)
        if half == 1 and start == 0:
            pairs = jnp.concatenate([fresh, pairs[CELLS:]], axis=0)
        scores = nt(queries, pairs)
        raised = jnp.maximum(highest, jnp.max(scores, axis=1, keepdims=True))
        factor = jnp.exp(highest - raised)
        weights = jnp.exp(scores - raised)
        denominator = denominator * factor + jnp.sum(weights, axis=1, keepdims=True)
        weighted = weighted * factor + nn(weights.astype(BF16), pairs)
        highest = raised
    attended = nn(order, (weighted / denominator).astype(BF16)).astype(BF16)
    own = nt(order, own_ref[...]).astype(BF16)
    pick = one_hot(iota((OC, C), 1) == iota((OC, C), 0) + at_ref[0] * OC, BF16)
    part = nt(attended, w_out_ref[...]) + nn(own, pick)
    part_ref[...] = part.astype(BF16).reshape(part_ref.shape)


def output_kernel(parts_ref, out_ref):
    total = jnp.sum(parts_ref[...].astype(F32), axis=0)
    for r in range(PC):
        out_ref[r] = total[PC * r : PC * (r + 1), :].astype(BF16)


def call(kernel, outs, scalars=0, outer=0, mib=8, space=pltpu.VMEM, scratch=()):
    def run(*args):
        args = list(args)
        for k in range(len(args) - outer, len(args)):
            args[k] = pltpu.with_memory_space_constraint(args[k], pltpu.HBM)
        specs = [pl.BlockSpec(memory_space=pltpu.SMEM)] * scalars
        specs += [pl.BlockSpec(memory_space=pltpu.VMEM)] * (len(args) - scalars - outer)
        specs += [pl.BlockSpec(memory_space=pltpu.HBM)] * outer
        return pl.pallas_call(
            kernel,
            out_shape=[
                pltpu.HBM(*out) if space is pltpu.HBM else jax.ShapeDtypeStruct(*out) for out in outs
            ],
            in_specs=specs,
            out_specs=[pl.BlockSpec(memory_space=space)] * len(outs),
            scratch_shapes=list(scratch),
            compiler_params=pltpu.CompilerParams(vmem_limit_bytes=mib * 2**20),
        )(*args)

    return run


def to_every(copies, axis):
    return lax.all_to_all(copies, axis, split_axis=0, concat_axis=0, tiled=True)


def swapped(inner, outer):
    pairs = [(i, j) for i in range(NS) if 0 <= (j := i + 1 if i % 2 else i - 1) < NS]
    outer = lax.ppermute(outer, PCOL, pairs)
    return lax.ppermute(inner, PCOL[-1], [(0, 1), (1, 0)]), outer


def shards(
    latent,
    norm_scale,
    norm_shift,
    time_shift,
    conv_bias,
    conv_one,
    conv_two,
    w_qkv,
    w_out,
    stale_kv,
):
    at = jnp.stack([lax.axis_index(PROW), lax.axis_index(PCOL)]).astype(jnp.int32)
    near = stale_kv.reshape(1, CELLS, 2 * HEAD)
    for step, (axis, bit) in enumerate(HOPS):
        count = lax.axis_size(axis)
        far = lax.ppermute(near, axis, [(i, i ^ bit) for i in range(count)])
        if step < len(HOPS) - 1:
            out = ((2 * near.shape[0], CELLS, 2 * HEAD), BF16)
            (near,) = call(
                join_kernel, [out], space=pltpu.HBM, scratch=[pltpu.SemaphoreType.DMA((2,))]
            )(near, far)
    sums_out = ((NS, 1, 128), F32)
    every = ((NP, OC, CELLS), BF16)
    tile = ((OC, CELLS), F32)
    edge = ((LR, C), BF16)
    (cols,) = call(columns_kernel, [((OC, 128), F32)], scalars=1)(
        at, norm_scale, norm_shift, conv_bias, time_shift.reshape(1, C)
    )

    def gathered(which, total, sums):
        sums = to_every(sums, PCOL)
        (copies,) = call(functools.partial(norm_kernel, which), [every])(total, sums, cols)
        return to_every(copies, PROW).reshape(C, CELLS)

    (block,) = call(
        pack_kernel,
        [((NP, BLOCK, 128), BF16)],
        outer=2,
        scratch=[
            pltpu.VMEM((PC, PC, C), BF16),
            pltpu.VMEM(w_out.shape, BF16),
            pltpu.SemaphoreType.DMA((2,)),
        ],
    )(latent, w_out)
    block = to_every(block, PROW)
    sums, inner, outer = call(stats_cells_kernel, [sums_out, edge, edge], scalars=1)(at, block)
    sums = to_every(sums, PCOL)
    inner, outer = swapped(inner, outer)
    (w_part,) = call(
        unpack_kernel,
        [((C, 128), BF16)],
        space=pltpu.HBM,
        scratch=[pltpu.VMEM((C, 128), BF16), pltpu.SemaphoreType.DMA],
    )(block)
    total, sums, own = call(conv_cells_kernel, [tile, sums_out, ((OC, CELLS), BF16)], scalars=1)(
        at,
        block,
        sums,
        norm_scale,
        norm_shift,
        conv_one.reshape(9 * OC, C),
        inner,
        outer,
        cols,
    )
    field = gathered(0, total, sums)
    mid, inner, outer = call(
        conv_channels_kernel, [tile, ((OC, LR), F32), ((OC, LR), F32)], scalars=1
    )(at, field, conv_two.reshape(9 * OC, C))
    inner, outer = swapped(inner, outer)
    resnet, sums = call(finish_kernel, [((OC, CELLS), BF16), sums_out], scalars=1)(
        at, mid, inner, outer, cols, own
    )
    field = gathered(1, resnet, sums)
    parts, fresh = call(
        attention_kernel,
        [((NP, NP, C), BF16), ((CELLS, 2 * HEAD), BF16)],
        scalars=1,
        outer=1,
        mib=16,
        scratch=[pltpu.VMEM((NS // 2, CELLS, 2 * HEAD), BF16), pltpu.SemaphoreType.DMA],
    )(at, field, w_qkv, w_part, resnet, far, near)
    (out,) = call(output_kernel, [((PC, PC, C), BF16)])(to_every(parts, PROW))
    return out, fresh.reshape(LR, PC, 1, 2 * HEAD)


def solution(mesh):
    torus = Mesh(
        mesh.devices.reshape(2, 8, 4, 4, 2), ("prow_0", "prow_1", "pcol_0", "pcol_1", "pcol_2")
    )
    in_specs = (
        P(PROW, PCOL, None),
        P(),
        P(),
        P(),
        P(),
        P(None, None, PROW, None),
        P(None, None, PROW, None),
        P(PROW, None),
        P(PROW, None),
        P(None, PCOL, PROW, None),
    )
    out_specs = (P(PROW, PCOL, None), P(None, PCOL, PROW, None))

    return jax.shard_map(
        shards, mesh=torus, in_specs=in_specs, out_specs=out_specs, check_vma=False
    )
```

```python
import functools

import jax
import jax.numpy as jnp
from jax import lax
from jax.experimental import pallas as pl
from jax.experimental.pallas import tpu as pltpu
from jax.sharding import Mesh
from jax.sharding import PartitionSpec as P

GROUPS = 32
HEAD = 64
PROW = ("prow_0", "prow_1")
PCOL = ("pcol_0", "pcol_1", "pcol_2")
HOPS = (("pcol_0", 1), ("pcol_0", 2), ("pcol_1", 1), ("pcol_1", 2), ("pcol_2", 1))
EPSILON = 1e-05
F32 = jnp.float32
BF16 = jnp.bfloat16

C = 1280
GC = C // GROUPS
NP = 16
NS = 32
LR = 64
PC = 4
CELLS = LR * PC
OC = C // NP
POPULATION = float(LR * PC * NS * GC)


def iota(shape, dim):
    return lax.broadcasted_iota(jnp.int32, shape, dim)


def one_hot(mask, dtype):
    return jnp.where(mask, 1.0, 0.0).astype(dtype)


def nt(left, right, precision=None):
    return lax.dot_general(
        left, right, (((1,), (1,)), ((), ())), precision=precision, preferred_element_type=F32
    )


def nn(left, right, precision=None):
    return lax.dot_general(
        left, right, (((1,), (0,)), ((), ())), precision=precision, preferred_element_type=F32
    )


def strip_order():
    o = iota((CELLS, CELLS), 0)
    i = iota((CELLS, CELLS), 1)
    return one_hot((o % LR) * PC + o // LR == i, BF16)


def cell_order():
    o = iota((CELLS, CELLS), 1)
    i = iota((CELLS, CELLS), 0)
    return one_hot((o % LR) * PC + o // LR == i, BF16)


ROWS = OC // 5 * C // 128
PIECE = 48
BLOCK = ROWS + PIECE


def moments(sums_ref):
    sums = jnp.sum(sums_ref[...], axis=0)
    mean = sums / POPULATION
    square = pltpu.roll(mean, 128 - GROUPS, 1)
    return mean, lax.rsqrt(jnp.maximum(square - mean * mean, 0.0) + EPSILON)


def silu(v):
    return v / (1.0 + jnp.exp(-v))


def pack_kernel(latent_hbm, w_hbm, out_ref, latent_ref, w_ref, sems):
    copies = [
        pltpu.make_async_copy(latent_hbm, latent_ref, sems.at[0]),
        pltpu.make_async_copy(w_hbm, w_ref, sems.at[1]),
    ]
    for copy in copies:
        copy.start()
    copies[0].wait()
    rows = [latent_ref[r].astype(F32) for r in range(PC)]
    patch = jnp.concatenate(rows, axis=0).astype(BF16)
    for j in range(C // 128):
        chunk = patch[:, 128 * j : 128 * (j + 1)]
        out_ref[:, NP * j : NP * (j + 1), :] = jnp.broadcast_to(chunk[None], (NP, NP, 128))
    copies[1].wait()
    lane = iota((PIECE, 128), 1)
    for k in range(NP // 2):
        w = w_ref[:, 128 * k : 128 * (k + 1)].astype(F32)
        turned = pltpu.roll(w, HEAD, 1)
        blank = jnp.zeros((2 * PIECE - OC, 128), F32)

        def halves(left, right):
            low = jnp.concatenate([right[PIECE:], blank], axis=0)
            return jnp.where(lane < HEAD, left[:PIECE], low).astype(BF16)

        out_ref[2 * k, ROWS:, :] = halves(w, turned)
        out_ref[2 * k + 1, ROWS:, :] = halves(turned, w)


def unpack_kernel(block_ref, out_hbm, out_ref, sem):
    lane = iota((PIECE, 128), 1)
    for p in range(NP):
        piece = block_ref[p, ROWS:, :].astype(F32)
        high = jnp.where(lane >= HEAD, pltpu.roll(piece, HEAD, 1), 0.0)
        low = jnp.where(lane >= HEAD, piece, 0.0)
        both = jnp.concatenate([high, low[: OC - PIECE]], axis=0)
        out_ref[OC * p : OC * (p + 1), :] = both.astype(BF16)
    copy = pltpu.make_async_copy(out_ref, out_hbm, sem)
    copy.start()
    copy.wait()


def columns_kernel(scale_ref, shift_ref, bias_ref, time_ref, out_ref):
    pick = iota((OC, C), 1) == iota((OC, C), 0) + lax.axis_index(PROW) * OC
    lane = iota((OC, 128), 1)
    total = jnp.zeros((OC, 128), F32)
    rows = [
        bias_ref[0:1, :] + time_ref[...],
        scale_ref[1:2, :],
        shift_ref[1:2, :],
        bias_ref[1:2, :],
        scale_ref[2:3, :],
        shift_ref[2:3, :],
    ]
    for k, row in enumerate(rows):
        col = jnp.sum(jnp.where(pick, row, 0.0), axis=1, keepdims=True)
        total = jnp.where(lane == k, col, total)
    out_ref[...] = total


def by_parity(one, other):
    even = lax.axis_index(PCOL) % 2 == 0
    return jnp.where(even, one, other), jnp.where(even, other, one)


def strip_chunk(block_ref, j):
    return block_ref[:, NP * j : NP * (j + 1), :].reshape(CELLS, 128)


def stats_cells_kernel(block_ref, out_ref, inner_ref, outer_ref):
    firsts, seconds = [], []
    row = iota((2 * LR, CELLS), 0)
    inner, outer = by_parity(PC - 1, 0)
    wanted = jnp.where(row < LR, row * PC + inner, (row - LR) * PC + outer)
    pick = one_hot(iota((2 * LR, CELLS), 1) == wanted, BF16)
    for j in range(C // 128):
        x = strip_chunk(block_ref, j)
        edges = nn(pick, x).astype(BF16)
        inner_ref[:, 128 * j : 128 * (j + 1)] = edges[:LR]
        outer_ref[:, 128 * j : 128 * (j + 1)] = edges[LR:]
        x = x.astype(F32)
        firsts.append(jnp.sum(x, axis=0, keepdims=True))
        seconds.append(jnp.sum(x * x, axis=0, keepdims=True))
    first = jnp.concatenate(firsts, axis=1)
    second = jnp.concatenate(seconds, axis=1)
    both = jnp.concatenate([first, second, jnp.zeros((6, C), F32)], axis=0)
    groups = one_hot(iota((C, 128), 0) // GC == iota((C, 128), 1), F32)
    reduced = nn(both, groups, lax.Precision.HIGHEST)
    row = reduced[0:1, :] + pltpu.roll(reduced, GROUPS, 1)[1:2, :]
    out_ref[...] = jnp.broadcast_to(row[None], out_ref.shape)


def tap_sums(products, b):
    row = iota((OC, products.shape[1]), 1) % LR
    above, here, below = (
        products[(3 * a + b) * OC : (3 * a + b + 1) * OC, :] for a in range(3)
    )
    above = jnp.where(row > 0, pltpu.roll(above, 1, 1), 0.0)
    below = jnp.where(row < LR - 1, pltpu.roll(below, products.shape[1] - 1, 1), 0.0)
    return here + above + below


def tap_columns(products):
    lane = iota((OC, CELLS), 1)
    before = tap_sums(products, 0)
    after = tap_sums(products, 2)
    mid = (
        tap_sums(products, 1)
        + jnp.where(lane >= LR, pltpu.roll(before, LR, 1), 0.0)
        + jnp.where(lane < CELLS - LR, pltpu.roll(after, CELLS - LR, 1), 0.0)
    )
    return before, mid, after


def with_sides(mid, left, right):
    blank = jnp.zeros((OC, CELLS - 2 * LR), F32)
    return mid + jnp.concatenate([left, blank, right], axis=1)


def conv_cells_kernel(
    block_ref,
    sums_ref,
    scale_ref,
    shift_ref,
    w_ref,
    inner_ref,
    outer_ref,
    cols_ref,
    total_ref,
    out_sums_ref,
    own_ref,
):
    mean, rstd = moments(sums_ref)
    both = jnp.concatenate([mean, rstd, jnp.zeros((6, 128), F32)], axis=0)
    groups = one_hot(iota((128, C), 1) // GC == iota((128, C), 0), F32)
    spread = nn(both, groups, lax.Precision.HIGHEST)
    gain = spread[1:2, :] * scale_ref[0:1, :]
    offset = shift_ref[0:1, :] - spread[0:1, :] * gain
    chunks = [strip_chunk(block_ref, j) for j in range(C // 128)]
    cells = nn(strip_order(), jnp.concatenate(chunks, axis=1))
    pick = one_hot(iota((OC, C), 1) == iota((OC, C), 0) + lax.axis_index(PROW) * OC, BF16)
    own_ref[...] = nt(pick, cells.astype(BF16)).astype(BF16)
    _, mid, _ = tap_columns(nt(w_ref[...], silu(cells * gain + offset).astype(BF16)))
    right, left = by_parity(inner_ref[...].astype(F32), outer_ref[...].astype(F32))
    sides = jnp.concatenate([left, right], axis=0)
    sides = silu(sides * gain + offset)
    row = iota((2 * LR, 1), 0)
    first = jnp.where(lax.axis_index(PCOL) > 0, 0, LR)
    last = jnp.where(lax.axis_index(PCOL) < NS - 1, 2 * LR, LR)
    sides = jnp.where((row >= first) & (row < last), sides, 0.0).astype(BF16)
    products = nt(w_ref[...], sides)
    left = tap_sums(products, 0)[:, :LR]
    right = tap_sums(products, 2)[:, LR:]
    total = with_sides(mid, left, right) + cols_ref[:, 0:1]
    total_ref[...] = total
    own_sums(total, out_sums_ref)


def conv_channels_kernel(x_ref, w_ref, mid_ref, inner_ref, outer_ref):
    before, mid, after = tap_columns(nn(w_ref[...], x_ref[...]))
    inner, outer = by_parity(before[:, CELLS - LR :], after[:, :LR])
    inner_ref[...] = inner
    outer_ref[...] = outer
    mid_ref[...] = mid


def whole(x):
    return jnp.sum(jnp.sum(x, axis=0, keepdims=True), axis=1, keepdims=True)


def own_sums(total, sums_ref):
    lane = iota((1, 128), 1)
    row = jnp.zeros((1, 128), F32)
    for k in range(2):
        half = total[GC * k : GC * (k + 1)]
        row = jnp.where(lane == k, whole(half), row)
        row = jnp.where(lane == k + GROUPS, whole(half * half), row)
    sums_ref[...] = jnp.broadcast_to(row[None], sums_ref.shape)


def finish_kernel(mid_ref, inner_ref, outer_ref, cols_ref, own_ref, total_ref, sums_ref):
    right, left = by_parity(inner_ref[...], outer_ref[...])
    total = with_sides(mid_ref[...], left, right)
    total = (own_ref[...].astype(F32) + total + cols_ref[:, 3:4]).astype(BF16)
    total_ref[...] = total
    own_sums(total.astype(F32), sums_ref)


def norm_kernel(which, total_ref, sums_ref, cols_ref, out_ref):
    mean, rstd = moments(sums_ref)
    upper = iota((OC, 1), 0) < GC
    gain = jnp.where(upper, rstd[:, 0:1], rstd[:, 1:2]) * cols_ref[:, 3 * which + 1 : 3 * which + 2]
    shift = cols_ref[:, 3 * which + 2 : 3 * which + 3]
    offset = shift - jnp.where(upper, mean[:, 0:1], mean[:, 1:2]) * gain
    value = total_ref[...].astype(F32) * gain + offset
    if which == 0:
        value = silu(value)
    out_ref[...] = jnp.broadcast_to(value.astype(BF16)[None], out_ref.shape)


def join_kernel(left_ref, right_ref, out_ref, sems):
    count = left_ref.shape[0]
    copies = [
        pltpu.make_async_copy(left_ref, out_ref.at[pl.ds(0, count)], sems.at[0]),
        pltpu.make_async_copy(right_ref, out_ref.at[pl.ds(count, count)], sems.at[1]),
    ]
    for copy in copies:
        copy.start()
    for copy in copies:
        copy.wait()


def attention_kernel(
    x_ref,
    w_ref,
    w_out_ref,
    own_ref,
    far_ref,
    near_hbm,
    part_ref,
    fresh_ref,
    near_ref,
    sem,
):
    chunk = 4
    copy = pltpu.make_async_copy(near_hbm, near_ref, sem)
    copy.start()
    mapped = nn(w_ref[...], x_ref[...])
    queries = jnp.transpose(mapped[:HEAD]).astype(BF16)
    fresh = jnp.transpose(mapped[HEAD:]).astype(BF16)
    queries = (queries.astype(F32) * HEAD ** (-0.5)).astype(BF16)
    queries = jnp.concatenate([queries, jnp.zeros((CELLS, HEAD), BF16)], axis=1)
    order = cell_order()
    fresh_ref[...] = nn(order, fresh).astype(BF16)
    highest = jnp.full((CELLS, 1), -jnp.inf, F32)
    denominator = jnp.zeros((CELLS, 1), F32)
    weighted = jnp.zeros((CELLS, 2 * HEAD), F32)
    for step in range(NS // chunk):
        half, start = divmod(chunk * step, NS // 2)
        if half == 1 and start == 0:
            copy.wait()
        pairs = (far_ref, near_ref)[half][start : start + chunk]
        pairs = pairs.reshape(chunk * CELLS, 2 * HEAD)
        if half == 1 and start == 0:
            pairs = jnp.concatenate([fresh, pairs[CELLS:]], axis=0)
        scores = nt(queries, pairs)
        raised = jnp.maximum(highest, jnp.max(scores, axis=1, keepdims=True))
        factor = jnp.exp(highest - raised)
        weights = jnp.exp(scores - raised)
        denominator = denominator * factor + jnp.sum(weights, axis=1, keepdims=True)
        weighted = weighted * factor + nn(weights.astype(BF16), pairs)
        highest = raised
    attended = nn(order, (weighted / denominator).astype(BF16)).astype(BF16)
    own = nt(order, own_ref[...]).astype(BF16)
    pick = one_hot(iota((OC, C), 1) == iota((OC, C), 0) + lax.axis_index(PROW) * OC, BF16)
    part = nt(attended, w_out_ref[...]) + nn(own, pick)
    part_ref[...] = part.astype(BF16).reshape(part_ref.shape)


def output_kernel(parts_ref, out_ref):
    total = jnp.sum(parts_ref[...].astype(F32), axis=0)
    for r in range(PC):
        out_ref[r] = total[PC * r : PC * (r + 1), :].astype(BF16)


def call(kernel, outs, outer=0, mib=8, space=pltpu.VMEM, scratch=()):
    def run(*args):
        args = list(args)
        for k in range(len(args) - outer, len(args)):
            args[k] = pltpu.with_memory_space_constraint(args[k], pltpu.HBM)
        specs = [pl.BlockSpec(memory_space=pltpu.VMEM)] * (len(args) - outer)
        specs += [pl.BlockSpec(memory_space=pltpu.HBM)] * outer
        return pl.pallas_call(
            kernel,
            out_shape=[
                pltpu.HBM(*out) if space is pltpu.HBM else jax.ShapeDtypeStruct(*out) for out in outs
            ],
            in_specs=specs,
            out_specs=[pl.BlockSpec(memory_space=space)] * len(outs),
            scratch_shapes=list(scratch),
            compiler_params=pltpu.CompilerParams(vmem_limit_bytes=mib * 2**20),
        )(*args)

    return run


def to_every(copies, axis):
    return lax.all_to_all(copies, axis, split_axis=0, concat_axis=0, tiled=True)


def swapped(inner, outer):
    pairs = [(i, j) for i in range(NS) if 0 <= (j := i + 1 if i % 2 else i - 1) < NS]
    outer = lax.ppermute(outer, PCOL, pairs)
    return lax.ppermute(inner, PCOL[-1], [(0, 1), (1, 0)]), outer


def shards(
    latent,
    norm_scale,
    norm_shift,
    time_shift,
    conv_bias,
    conv_one,
    conv_two,
    w_qkv,
    w_out,
    stale_kv,
):
    near = stale_kv.reshape(1, CELLS, 2 * HEAD)
    for step, (axis, bit) in enumerate(HOPS):
        count = lax.axis_size(axis)
        far = lax.ppermute(near, axis, [(i, i ^ bit) for i in range(count)])
        if step < len(HOPS) - 1:
            out = ((2 * near.shape[0], CELLS, 2 * HEAD), BF16)
            (near,) = call(
                join_kernel, [out], space=pltpu.HBM, scratch=[pltpu.SemaphoreType.DMA((2,))]
            )(near, far)
    sums_out = ((NS, 1, 128), F32)
    every = ((NP, OC, CELLS), BF16)
    tile = ((OC, CELLS), F32)
    edge = ((LR, C), BF16)
    (cols,) = call(columns_kernel, [((OC, 128), F32)])(
        norm_scale, norm_shift, conv_bias, time_shift.reshape(1, C)
    )

    def gathered(which, total, sums):
        sums = to_every(sums, PCOL)
        (copies,) = call(functools.partial(norm_kernel, which), [every])(total, sums, cols)
        return to_every(copies, PROW).reshape(C, CELLS)

    (block,) = call(
        pack_kernel,
        [((NP, BLOCK, 128), BF16)],
        outer=2,
        scratch=[
            pltpu.VMEM((PC, PC, C), BF16),
            pltpu.VMEM(w_out.shape, BF16),
            pltpu.SemaphoreType.DMA((2,)),
        ],
    )(latent, w_out)
    block = to_every(block, PROW)
    sums, inner, outer = call(stats_cells_kernel, [sums_out, edge, edge])(block)
    sums = to_every(sums, PCOL)
    inner, outer = swapped(inner, outer)
    (w_part,) = call(
        unpack_kernel,
        [((C, 128), BF16)],
        space=pltpu.HBM,
        scratch=[pltpu.VMEM((C, 128), BF16), pltpu.SemaphoreType.DMA],
    )(block)
    total, sums, own = call(conv_cells_kernel, [tile, sums_out, ((OC, CELLS), BF16)])(
        block,
        sums,
        norm_scale,
        norm_shift,
        conv_one.reshape(9 * OC, C),
        inner,
        outer,
        cols,
    )
    field = gathered(0, total, sums)
    mid, inner, outer = call(
        conv_channels_kernel, [tile, ((OC, LR), F32), ((OC, LR), F32)]
    )(field, conv_two.reshape(9 * OC, C))
    inner, outer = swapped(inner, outer)
    resnet, sums = call(finish_kernel, [((OC, CELLS), BF16), sums_out])(
        mid, inner, outer, cols, own
    )
    field = gathered(1, resnet, sums)
    parts, fresh = call(
        attention_kernel,
        [((NP, NP, C), BF16), ((CELLS, 2 * HEAD), BF16)],
        outer=1,
        mib=16,
        scratch=[pltpu.VMEM((NS // 2, CELLS, 2 * HEAD), BF16), pltpu.SemaphoreType.DMA],
    )(field, w_qkv, w_part, resnet, far, near)
    (out,) = call(output_kernel, [((PC, PC, C), BF16)])(to_every(parts, PROW))
    return out, fresh.reshape(LR, PC, 1, 2 * HEAD)


def solution(mesh):
    torus = Mesh(
        mesh.devices.reshape(2, 8, 4, 4, 2), ("prow_0", "prow_1", "pcol_0", "pcol_1", "pcol_2")
    )
    in_specs = (
        P(PROW, PCOL, None),
        P(),
        P(),
        P(),
        P(),
        P(None, None, PROW, None),
        P(None, None, PROW, None),
        P(PROW, None),
        P(PROW, None),
        P(None, PCOL, PROW, None),
    )
    out_specs = (P(PROW, PCOL, None), P(None, PCOL, PROW, None))

    return jax.shard_map(
        shards, mesh=torus, in_specs=in_specs, out_specs=out_specs, check_vma=False
    )
```

```python
import functools

import jax
import jax.numpy as jnp
from jax import lax
from jax.experimental import pallas as pl
from jax.experimental.pallas import tpu as pltpu
from jax.sharding import Mesh
from jax.sharding import PartitionSpec as P

GROUPS = 32
HEAD = 64
PROW = ("prow_0", "prow_1")
PCOL = ("pcol_0", "pcol_1", "pcol_2")
HOPS = (("pcol_0", 1), ("pcol_0", 2), ("pcol_1", 1), ("pcol_1", 2), ("pcol_2", 1))
EPSILON = 1e-05
F32 = jnp.float32
BF16 = jnp.bfloat16

C = 1280
GC = C // GROUPS
NP = 16
NS = 32
LR = 64
PC = 4
CELLS = LR * PC
OC = C // NP
POPULATION = float(LR * PC * NS * GC)


def iota(shape, dim):
    return lax.broadcasted_iota(jnp.int32, shape, dim)


def one_hot(mask, dtype):
    return jnp.where(mask, 1.0, 0.0).astype(dtype)


def nt(left, right, precision=None):
    return lax.dot_general(
        left, right, (((1,), (1,)), ((), ())), precision=precision, preferred_element_type=F32
    )


def nn(left, right, precision=None):
    return lax.dot_general(
        left, right, (((1,), (0,)), ((), ())), precision=precision, preferred_element_type=F32
    )


def strip_order():
    o = iota((CELLS, CELLS), 0)
    i = iota((CELLS, CELLS), 1)
    return one_hot((o % LR) * PC + o // LR == i, BF16)


def cell_order():
    o = iota((CELLS, CELLS), 1)
    i = iota((CELLS, CELLS), 0)
    return one_hot((o % LR) * PC + o // LR == i, BF16)


ROWS = OC // 5 * C // 128
PIECE = 48
BLOCK = ROWS + PIECE


def moments(sums_ref):
    sums = jnp.sum(sums_ref[...], axis=0)
    mean = sums / POPULATION
    square = pltpu.roll(mean, 128 - GROUPS, 1)
    return mean, lax.rsqrt(jnp.maximum(square - mean * mean, 0.0) + EPSILON)


def silu(v):
    return v / (1.0 + jnp.exp(-v))


def pack_kernel(latent_hbm, w_hbm, out_hbm, latent_ref, w_ref, patch_ref, piece_ref, sems):
    copies = [
        pltpu.make_async_copy(latent_hbm, latent_ref, sems.at[0]),
        pltpu.make_async_copy(w_hbm, w_ref, sems.at[1]),
    ]
    for copy in copies:
        copy.start()
    copies[0].wait()
    rows = [latent_ref[r].astype(F32) for r in range(PC)]
    patch = jnp.concatenate(rows, axis=0).astype(BF16)
    for j in range(C // 128):
        patch_ref[NP * j : NP * (j + 1), :] = patch[:, 128 * j : 128 * (j + 1)]
    for k in range(NP):
        copies.append(
            pltpu.make_async_copy(patch_ref, out_hbm.at[k, pl.ds(0, ROWS)], sems.at[2 + k])
        )
        copies[-1].start()
    copies[1].wait()
    lane = iota((PIECE, 128), 1)
    for k in range(NP // 2):
        w = w_ref[:, 128 * k : 128 * (k + 1)].astype(F32)
        turned = pltpu.roll(w, HEAD, 1)
        blank = jnp.zeros((2 * PIECE - OC, 128), F32)

        def halves(left, right):
            low = jnp.concatenate([right[PIECE:], blank], axis=0)
            return jnp.where(lane < HEAD, left[:PIECE], low).astype(BF16)

        piece_ref[2 * k] = halves(w, turned)
        piece_ref[2 * k + 1] = halves(turned, w)
    for k in range(NP):
        copies.append(
            pltpu.make_async_copy(
                piece_ref.at[k], out_hbm.at[k, pl.ds(ROWS, PIECE)], sems.at[2 + NP + k]
            )
        )
        copies[-1].start()
    for copy in copies[2:]:
        copy.wait()


def unpack_kernel(block_ref, out_hbm, out_ref, sem):
    lane = iota((PIECE, 128), 1)
    for p in range(NP):
        piece = block_ref[p, ROWS:, :].astype(F32)
        high = jnp.where(lane >= HEAD, pltpu.roll(piece, HEAD, 1), 0.0)
        low = jnp.where(lane >= HEAD, piece, 0.0)
        both = jnp.concatenate([high, low[: OC - PIECE]], axis=0)
        out_ref[OC * p : OC * (p + 1), :] = both.astype(BF16)
    copy = pltpu.make_async_copy(out_ref, out_hbm, sem)
    copy.start()
    copy.wait()


def columns_kernel(scale_ref, shift_ref, bias_ref, time_ref, out_ref):
    pick = iota((OC, C), 1) == iota((OC, C), 0) + lax.axis_index(PROW) * OC
    lane = iota((OC, 128), 1)
    total = jnp.zeros((OC, 128), F32)
    rows = [
        bias_ref[0:1, :] + time_ref[...],
        scale_ref[1:2, :],
        shift_ref[1:2, :],
        bias_ref[1:2, :],
        scale_ref[2:3, :],
        shift_ref[2:3, :],
    ]
    for k, row in enumerate(rows):
        col = jnp.sum(jnp.where(pick, row, 0.0), axis=1, keepdims=True)
        total = jnp.where(lane == k, col, total)
    out_ref[...] = total


def by_parity(one, other):
    even = lax.axis_index(PCOL) % 2 == 0
    return jnp.where(even, one, other), jnp.where(even, other, one)


def strip_chunk(block_ref, j):
    return block_ref[:, NP * j : NP * (j + 1), :].reshape(CELLS, 128)


def stats_cells_kernel(block_ref, out_ref, inner_ref, outer_ref):
    firsts, seconds = [], []
    row = iota((2 * LR, CELLS), 0)
    inner, outer = by_parity(PC - 1, 0)
    wanted = jnp.where(row < LR, row * PC + inner, (row - LR) * PC + outer)
    pick = one_hot(iota((2 * LR, CELLS), 1) == wanted, BF16)
    for j in range(C // 128):
        x = strip_chunk(block_ref, j)
        edges = nn(pick, x).astype(BF16)
        inner_ref[:, 128 * j : 128 * (j + 1)] = edges[:LR]
        outer_ref[:, 128 * j : 128 * (j + 1)] = edges[LR:]
        x = x.astype(F32)
        firsts.append(jnp.sum(x, axis=0, keepdims=True))
        seconds.append(jnp.sum(x * x, axis=0, keepdims=True))
    first = jnp.concatenate(firsts, axis=1)
    second = jnp.concatenate(seconds, axis=1)
    both = jnp.concatenate([first, second, jnp.zeros((6, C), F32)], axis=0)
    groups = one_hot(iota((C, 128), 0) // GC == iota((C, 128), 1), F32)
    reduced = nn(both, groups, lax.Precision.HIGHEST)
    row = reduced[0:1, :] + pltpu.roll(reduced, GROUPS, 1)[1:2, :]
    out_ref[...] = jnp.broadcast_to(row[None], out_ref.shape)


def tap_sums(products, b):
    row = iota((OC, products.shape[1]), 1) % LR
    above, here, below = (
        products[(3 * a + b) * OC : (3 * a + b + 1) * OC, :] for a in range(3)
    )
    above = jnp.where(row > 0, pltpu.roll(above, 1, 1), 0.0)
    below = jnp.where(row < LR - 1, pltpu.roll(below, products.shape[1] - 1, 1), 0.0)
    return here + above + below


def tap_columns(products):
    lane = iota((OC, CELLS), 1)
    before = tap_sums(products, 0)
    after = tap_sums(products, 2)
    mid = (
        tap_sums(products, 1)
        + jnp.where(lane >= LR, pltpu.roll(before, LR, 1), 0.0)
        + jnp.where(lane < CELLS - LR, pltpu.roll(after, CELLS - LR, 1), 0.0)
    )
    return before, mid, after


def with_sides(mid, left, right):
    blank = jnp.zeros((OC, CELLS - 2 * LR), F32)
    return mid + jnp.concatenate([left, blank, right], axis=1)


def conv_cells_kernel(
    block_ref,
    sums_ref,
    scale_ref,
    shift_ref,
    w_ref,
    inner_ref,
    outer_ref,
    cols_ref,
    total_ref,
    out_sums_ref,
    own_ref,
):
    mean, rstd = moments(sums_ref)
    both = jnp.concatenate([mean, rstd, jnp.zeros((6, 128), F32)], axis=0)
    groups = one_hot(iota((128, C), 1) // GC == iota((128, C), 0), F32)
    spread = nn(both, groups, lax.Precision.HIGHEST)
    gain = spread[1:2, :] * scale_ref[0:1, :]
    offset = shift_ref[0:1, :] - spread[0:1, :] * gain
    chunks = [strip_chunk(block_ref, j) for j in range(C // 128)]
    cells = nn(strip_order(), jnp.concatenate(chunks, axis=1))
    pick = one_hot(iota((OC, C), 1) == iota((OC, C), 0) + lax.axis_index(PROW) * OC, BF16)
    own_ref[...] = nt(pick, cells.astype(BF16)).astype(BF16)
    _, mid, _ = tap_columns(nt(w_ref[...], silu(cells * gain + offset).astype(BF16)))
    right, left = by_parity(inner_ref[...].astype(F32), outer_ref[...].astype(F32))
    sides = jnp.concatenate([left, right], axis=0)
    sides = silu(sides * gain + offset)
    row = iota((2 * LR, 1), 0)
    first = jnp.where(lax.axis_index(PCOL) > 0, 0, LR)
    last = jnp.where(lax.axis_index(PCOL) < NS - 1, 2 * LR, LR)
    sides = jnp.where((row >= first) & (row < last), sides, 0.0).astype(BF16)
    products = nt(w_ref[...], sides)
    left = tap_sums(products, 0)[:, :LR]
    right = tap_sums(products, 2)[:, LR:]
    total = with_sides(mid, left, right) + cols_ref[:, 0:1]
    total_ref[...] = total
    own_sums(total, out_sums_ref)


def conv_channels_kernel(x_ref, w_ref, mid_ref, inner_ref, outer_ref):
    before, mid, after = tap_columns(nn(w_ref[...], x_ref[...]))
    inner, outer = by_parity(before[:, CELLS - LR :], after[:, :LR])
    inner_ref[...] = inner
    outer_ref[...] = outer
    mid_ref[...] = mid


def whole(x):
    return jnp.sum(jnp.sum(x, axis=0, keepdims=True), axis=1, keepdims=True)


def own_sums(total, sums_ref):
    lane = iota((1, 128), 1)
    row = jnp.zeros((1, 128), F32)
    for k in range(2):
        half = total[GC * k : GC * (k + 1)]
        row = jnp.where(lane == k, whole(half), row)
        row = jnp.where(lane == k + GROUPS, whole(half * half), row)
    sums_ref[...] = jnp.broadcast_to(row[None], sums_ref.shape)


def finish_kernel(mid_ref, inner_ref, outer_ref, cols_ref, own_ref, total_ref, sums_ref):
    right, left = by_parity(inner_ref[...], outer_ref[...])
    total = with_sides(mid_ref[...], left, right)
    total = (own_ref[...].astype(F32) + total + cols_ref[:, 3:4]).astype(BF16)
    total_ref[...] = total
    own_sums(total.astype(F32), sums_ref)


def norm_kernel(which, total_ref, sums_ref, cols_ref, out_hbm, out_ref, sems):
    mean, rstd = moments(sums_ref)
    upper = iota((OC, 1), 0) < GC
    gain = jnp.where(upper, rstd[:, 0:1], rstd[:, 1:2]) * cols_ref[:, 3 * which + 1 : 3 * which + 2]
    shift = cols_ref[:, 3 * which + 2 : 3 * which + 3]
    offset = shift - jnp.where(upper, mean[:, 0:1], mean[:, 1:2]) * gain
    value = total_ref[...].astype(F32) * gain + offset
    if which == 0:
        value = silu(value)
    out_ref[...] = value.astype(BF16)
    copies = [pltpu.make_async_copy(out_ref, out_hbm.at[k], sems.at[k]) for k in range(NP)]
    for copy in copies:
        copy.start()
    for copy in copies:
        copy.wait()


def join_kernel(left_ref, right_ref, out_ref, sems):
    count = left_ref.shape[0]
    copies = [
        pltpu.make_async_copy(left_ref, out_ref.at[pl.ds(0, count)], sems.at[0]),
        pltpu.make_async_copy(right_ref, out_ref.at[pl.ds(count, count)], sems.at[1]),
    ]
    for copy in copies:
        copy.start()
    for copy in copies:
        copy.wait()


def attention_kernel(
    x_ref,
    w_ref,
    w_out_ref,
    own_ref,
    far_ref,
    near_hbm,
    part_ref,
    fresh_ref,
    near_ref,
    sem,
):
    chunk = 8
    copy = pltpu.make_async_copy(near_hbm, near_ref, sem)
    copy.start()
    mapped = nn(w_ref[...], x_ref[...])
    queries = jnp.transpose(mapped[:HEAD]).astype(BF16)
    fresh = jnp.transpose(mapped[HEAD:]).astype(BF16)
    queries = (queries.astype(F32) * HEAD ** (-0.5)).astype(BF16)
    queries = jnp.concatenate([queries, jnp.zeros((CELLS, HEAD), BF16)], axis=1)
    order = cell_order()
    fresh_ref[...] = nn(order, fresh).astype(BF16)
    highest = jnp.full((CELLS, 1), -jnp.inf, F32)
    denominator = jnp.zeros((CELLS, 1), F32)
    weighted = jnp.zeros((CELLS, 2 * HEAD), F32)
    for step in range(NS // chunk):
        half, start = divmod(chunk * step, NS // 2)
        if half == 1 and start == 0:
            copy.wait()
        pairs = (far_ref, near_ref)[half][start : start + chunk]
        pairs = pairs.reshape(chunk * CELLS, 2 * HEAD)
        if half == 1 and start == 0:
            pairs = jnp.concatenate([fresh, pairs[CELLS:]], axis=0)
        scores = nt(queries, pairs)
        raised = jnp.maximum(highest, jnp.max(scores, axis=1, keepdims=True))
        factor = jnp.exp(highest - raised)
        weights = jnp.exp(scores - raised)
        denominator = denominator * factor + jnp.sum(weights, axis=1, keepdims=True)
        weighted = weighted * factor + nn(weights.astype(BF16), pairs)
        highest = raised
    attended = nn(order, (weighted / denominator).astype(BF16)).astype(BF16)
    own = nt(order, own_ref[...]).astype(BF16)
    pick = one_hot(iota((OC, C), 1) == iota((OC, C), 0) + lax.axis_index(PROW) * OC, BF16)
    part = nt(attended, w_out_ref[...]) + nn(own, pick)
    part_ref[...] = part.astype(BF16).reshape(part_ref.shape)


def output_kernel(parts_ref, out_ref):
    total = jnp.sum(parts_ref[...].astype(F32), axis=0)
    for r in range(PC):
        out_ref[r] = total[PC * r : PC * (r + 1), :].astype(BF16)


def call(kernel, outs, outer=0, mib=8, space=pltpu.VMEM, scratch=()):
    def run(*args):
        args = list(args)
        for k in range(len(args) - outer, len(args)):
            args[k] = pltpu.with_memory_space_constraint(args[k], pltpu.HBM)
        specs = [pl.BlockSpec(memory_space=pltpu.VMEM)] * (len(args) - outer)
        specs += [pl.BlockSpec(memory_space=pltpu.HBM)] * outer
        return pl.pallas_call(
            kernel,
            out_shape=[
                pltpu.HBM(*out) if space is pltpu.HBM else jax.ShapeDtypeStruct(*out) for out in outs
            ],
            in_specs=specs,
            out_specs=[pl.BlockSpec(memory_space=space)] * len(outs),
            scratch_shapes=list(scratch),
            compiler_params=pltpu.CompilerParams(vmem_limit_bytes=mib * 2**20),
        )(*args)

    return run


def to_every(copies, axis):
    return lax.all_to_all(copies, axis, split_axis=0, concat_axis=0, tiled=True)


def swapped(inner, outer):
    pairs = [(i, j) for i in range(NS) if 0 <= (j := i + 1 if i % 2 else i - 1) < NS]
    outer = lax.ppermute(outer, PCOL, pairs)
    return lax.ppermute(inner, PCOL[-1], [(0, 1), (1, 0)]), outer


def shards(
    latent,
    norm_scale,
    norm_shift,
    time_shift,
    conv_bias,
    conv_one,
    conv_two,
    w_qkv,
    w_out,
    stale_kv,
):
    near = stale_kv.reshape(1, CELLS, 2 * HEAD)
    for step, (axis, bit) in enumerate(HOPS):
        count = lax.axis_size(axis)
        far = lax.ppermute(near, axis, [(i, i ^ bit) for i in range(count)])
        if step < len(HOPS) - 1:
            out = ((2 * near.shape[0], CELLS, 2 * HEAD), BF16)
            (near,) = call(
                join_kernel, [out], space=pltpu.HBM, scratch=[pltpu.SemaphoreType.DMA((2,))]
            )(near, far)
    sums_out = ((NS, 1, 128), F32)
    every = ((NP, OC, CELLS), BF16)
    tile = ((OC, CELLS), F32)
    edge = ((LR, C), BF16)
    (cols,) = call(columns_kernel, [((OC, 128), F32)])(
        norm_scale, norm_shift, conv_bias, time_shift.reshape(1, C)
    )

    def gathered(which, total, sums):
        sums = to_every(sums, PCOL)
        (copies,) = call(
            functools.partial(norm_kernel, which),
            [every],
            space=pltpu.HBM,
            scratch=[pltpu.VMEM((OC, CELLS), BF16), pltpu.SemaphoreType.DMA((NP,))],
        )(
            total, sums, cols
        )
        return to_every(copies, PROW).reshape(C, CELLS)

    (block,) = call(
        pack_kernel,
        [((NP, BLOCK, 128), BF16)],
        outer=2,
        scratch=[
            pltpu.VMEM((PC, PC, C), BF16),
            pltpu.VMEM(w_out.shape, BF16),
            pltpu.VMEM((ROWS, 128), BF16),
            pltpu.VMEM((NP, PIECE, 128), BF16),
            pltpu.SemaphoreType.DMA((2 + 2 * NP,)),
        ],
        space=pltpu.HBM,
    )(latent, w_out)
    block = to_every(block, PROW)
    sums, inner, outer = call(stats_cells_kernel, [sums_out, edge, edge])(block)
    sums = to_every(sums, PCOL)
    inner, outer = swapped(inner, outer)
    (w_part,) = call(
        unpack_kernel,
        [((C, 128), BF16)],
        space=pltpu.HBM,
        scratch=[pltpu.VMEM((C, 128), BF16), pltpu.SemaphoreType.DMA],
    )(block)
    total, sums, own = call(conv_cells_kernel, [tile, sums_out, ((OC, CELLS), BF16)])(
        block,
        sums,
        norm_scale,
        norm_shift,
        conv_one.reshape(9 * OC, C),
        inner,
        outer,
        cols,
    )
    field = gathered(0, total, sums)
    mid, inner, outer = call(
        conv_channels_kernel, [tile, ((OC, LR), F32), ((OC, LR), F32)]
    )(field, conv_two.reshape(9 * OC, C))
    inner, outer = swapped(inner, outer)
    resnet, sums = call(finish_kernel, [((OC, CELLS), BF16), sums_out])(
        mid, inner, outer, cols, own
    )
    field = gathered(1, resnet, sums)
    parts, fresh = call(
        attention_kernel,
        [((NP, NP, C), BF16), ((CELLS, 2 * HEAD), BF16)],
        outer=1,
        mib=16,
        scratch=[pltpu.VMEM((NS // 2, CELLS, 2 * HEAD), BF16), pltpu.SemaphoreType.DMA],
    )(field, w_qkv, w_part, resnet, far, near)
    (out,) = call(output_kernel, [((PC, PC, C), BF16)])(to_every(parts, PROW))
    return out, fresh.reshape(LR, PC, 1, 2 * HEAD)


def solution(mesh):
    torus = Mesh(
        mesh.devices.reshape(2, 8, 4, 4, 2), ("prow_0", "prow_1", "pcol_0", "pcol_1", "pcol_2")
    )
    in_specs = (
        P(PROW, PCOL, None),
        P(),
        P(),
        P(),
        P(),
        P(None, None, PROW, None),
        P(None, None, PROW, None),
        P(PROW, None),
        P(PROW, None),
        P(None, PCOL, PROW, None),
    )
    out_specs = (P(PROW, PCOL, None), P(None, PCOL, PROW, None))

    return jax.shard_map(
        shards, mesh=torus, in_specs=in_specs, out_specs=out_specs, check_vma=False
    )
```

```python
import functools

import jax
import jax.numpy as jnp
from jax import lax
from jax.experimental import pallas as pl
from jax.experimental.pallas import tpu as pltpu
from jax.sharding import Mesh
from jax.sharding import PartitionSpec as P

GROUPS = 32
HEAD = 64
PROW = ("prow_0", "prow_1")
PCOL = ("pcol_0", "pcol_1", "pcol_2")
HOPS = (("pcol_0", 1), ("pcol_0", 2), ("pcol_1", 1), ("pcol_1", 2), ("pcol_2", 1))
EPSILON = 1e-05
F32 = jnp.float32
BF16 = jnp.bfloat16

C = 1280
GC = C // GROUPS
NP = 16
NS = 32
LR = 64
PC = 4
CELLS = LR * PC
OC = C // NP
POPULATION = float(LR * PC * NS * GC)


def iota(shape, dim):
    return lax.broadcasted_iota(jnp.int32, shape, dim)


def one_hot(mask, dtype):
    return jnp.where(mask, 1.0, 0.0).astype(dtype)


def nt(left, right, precision=None):
    return lax.dot_general(
        left, right, (((1,), (1,)), ((), ())), precision=precision, preferred_element_type=F32
    )


def nn(left, right, precision=None):
    return lax.dot_general(
        left, right, (((1,), (0,)), ((), ())), precision=precision, preferred_element_type=F32
    )


def strip_order():
    o = iota((CELLS, CELLS), 0)
    i = iota((CELLS, CELLS), 1)
    return one_hot((o % LR) * PC + o // LR == i, BF16)


def cell_order():
    o = iota((CELLS, CELLS), 1)
    i = iota((CELLS, CELLS), 0)
    return one_hot((o % LR) * PC + o // LR == i, BF16)


ROWS = OC // 5 * C // 128
PIECE = 40
BLOCK = ROWS + PIECE


def moments(sums_ref):
    sums = jnp.sum(sums_ref[...], axis=0)
    mean = sums / POPULATION
    square = pltpu.roll(mean, 128 - GROUPS, 1)
    return mean, lax.rsqrt(jnp.maximum(square - mean * mean, 0.0) + EPSILON)


def silu(v):
    return v / (1.0 + jnp.exp(-v))


def pack_kernel(latent_hbm, w_hbm, out_ref, latent_ref, w_ref, sems):
    copies = [
        pltpu.make_async_copy(latent_hbm, latent_ref, sems.at[0]),
        pltpu.make_async_copy(w_hbm, w_ref, sems.at[1]),
    ]
    for copy in copies:
        copy.start()
    copies[0].wait()
    rows = [latent_ref[r].astype(F32) for r in range(PC)]
    patch = jnp.concatenate(rows, axis=0).astype(BF16)
    for j in range(C // 128):
        chunk = patch[:, 128 * j : 128 * (j + 1)]
        out_ref[:, NP * j : NP * (j + 1), :] = jnp.broadcast_to(chunk[None], (NP, NP, 128))
    copies[1].wait()
    lane = iota((PIECE, 128), 1)
    for k in range(NP // 2):
        w = w_ref[:, 128 * k : 128 * (k + 1)].astype(F32)
        turned = pltpu.roll(w, HEAD, 1)

        def halves(left, right):
            return jnp.where(lane < HEAD, left[:PIECE], right[PIECE:]).astype(BF16)

        out_ref[2 * k, ROWS:, :] = halves(w, turned)
        out_ref[2 * k + 1, ROWS:, :] = halves(turned, w)


def unpack_kernel(block_ref, out_hbm, out_ref, sem):
    lane = iota((PIECE, 128), 1)
    for p in range(NP):
        piece = block_ref[p, ROWS:, :].astype(F32)
        high = jnp.where(lane >= HEAD, pltpu.roll(piece, HEAD, 1), 0.0)
        low = jnp.where(lane >= HEAD, piece, 0.0)
        both = jnp.concatenate([high, low], axis=0)
        out_ref[OC * p : OC * (p + 1), :] = both.astype(BF16)
    copy = pltpu.make_async_copy(out_ref, out_hbm, sem)
    copy.start()
    copy.wait()


def columns_kernel(scale_ref, shift_ref, bias_ref, time_ref, out_ref):
    pick = iota((OC, C), 1) == iota((OC, C), 0) + lax.axis_index(PROW) * OC
    lane = iota((OC, 128), 1)
    total = jnp.zeros((OC, 128), F32)
    rows = [
        bias_ref[0:1, :] + time_ref[...],
        scale_ref[1:2, :],
        shift_ref[1:2, :],
        bias_ref[1:2, :],
        scale_ref[2:3, :],
        shift_ref[2:3, :],
    ]
    for k, row in enumerate(rows):
        col = jnp.sum(jnp.where(pick, row, 0.0), axis=1, keepdims=True)
        total = jnp.where(lane == k, col, total)
    out_ref[...] = total


def by_parity(one, other):
    even = lax.axis_index(PCOL) % 2 == 0
    return jnp.where(even, one, other), jnp.where(even, other, one)


def strip_chunk(block_ref, j):
    return block_ref[:, NP * j : NP * (j + 1), :].reshape(CELLS, 128)


def stats_cells_kernel(block_ref, out_ref, inner_ref, outer_ref):
    firsts, seconds = [], []
    row = iota((2 * LR, CELLS), 0)
    inner, outer = by_parity(PC - 1, 0)
    wanted = jnp.where(row < LR, row * PC + inner, (row - LR) * PC + outer)
    pick = one_hot(iota((2 * LR, CELLS), 1) == wanted, BF16)
    for j in range(C // 128):
        x = strip_chunk(block_ref, j)
        edges = nn(pick, x).astype(BF16)
        inner_ref[:, 128 * j : 128 * (j + 1)] = edges[:LR]
        outer_ref[:, 128 * j : 128 * (j + 1)] = edges[LR:]
        x = x.astype(F32)
        firsts.append(jnp.sum(x, axis=0, keepdims=True))
        seconds.append(jnp.sum(x * x, axis=0, keepdims=True))
    first = jnp.concatenate(firsts, axis=1)
    second = jnp.concatenate(seconds, axis=1)
    both = jnp.concatenate([first, second, jnp.zeros((6, C), F32)], axis=0)
    groups = one_hot(iota((C, 128), 0) // GC == iota((C, 128), 1), F32)
    reduced = nn(both, groups, lax.Precision.HIGHEST)
    row = reduced[0:1, :] + pltpu.roll(reduced, GROUPS, 1)[1:2, :]
    out_ref[...] = jnp.broadcast_to(row[None], out_ref.shape)


def tap_sums(products, b):
    row = iota((OC, products.shape[1]), 1) % LR
    above, here, below = (
        products[(3 * a + b) * OC : (3 * a + b + 1) * OC, :] for a in range(3)
    )
    above = jnp.where(row > 0, pltpu.roll(above, 1, 1), 0.0)
    below = jnp.where(row < LR - 1, pltpu.roll(below, products.shape[1] - 1, 1), 0.0)
    return here + above + below


def tap_columns(products):
    lane = iota((OC, CELLS), 1)
    before = tap_sums(products, 0)
    after = tap_sums(products, 2)
    mid = (
        tap_sums(products, 1)
        + jnp.where(lane >= LR, pltpu.roll(before, LR, 1), 0.0)
        + jnp.where(lane < CELLS - LR, pltpu.roll(after, CELLS - LR, 1), 0.0)
    )
    return before, mid, after


def with_sides(mid, left, right):
    blank = jnp.zeros((OC, CELLS - 2 * LR), F32)
    return mid + jnp.concatenate([left, blank, right], axis=1)


def conv_cells_kernel(
    block_ref,
    sums_ref,
    scale_ref,
    shift_ref,
    w_ref,
    inner_ref,
    outer_ref,
    cols_ref,
    total_ref,
    out_sums_ref,
    own_ref,
):
    mean, rstd = moments(sums_ref)
    both = jnp.concatenate([mean, rstd, jnp.zeros((6, 128), F32)], axis=0)
    groups = one_hot(iota((128, C), 1) // GC == iota((128, C), 0), F32)
    spread = nn(both, groups, lax.Precision.HIGHEST)
    gain = spread[1:2, :] * scale_ref[0:1, :]
    offset = shift_ref[0:1, :] - spread[0:1, :] * gain
    chunks = [strip_chunk(block_ref, j) for j in range(C // 128)]
    cells = nn(strip_order(), jnp.concatenate(chunks, axis=1))
    pick = one_hot(iota((OC, C), 1) == iota((OC, C), 0) + lax.axis_index(PROW) * OC, BF16)
    own_ref[...] = nt(pick, cells.astype(BF16)).astype(BF16)
    _, mid, _ = tap_columns(nt(w_ref[...], silu(cells * gain + offset).astype(BF16)))
    right, left = by_parity(inner_ref[...].astype(F32), outer_ref[...].astype(F32))
    sides = jnp.concatenate([left, right], axis=0)
    sides = silu(sides * gain + offset)
    row = iota((2 * LR, 1), 0)
    first = jnp.where(lax.axis_index(PCOL) > 0, 0, LR)
    last = jnp.where(lax.axis_index(PCOL) < NS - 1, 2 * LR, LR)
    sides = jnp.where((row >= first) & (row < last), sides, 0.0).astype(BF16)
    products = nt(w_ref[...], sides)
    left = tap_sums(products, 0)[:, :LR]
    right = tap_sums(products, 2)[:, LR:]
    total = with_sides(mid, left, right) + cols_ref[:, 0:1]
    total_ref[...] = total
    own_sums(total, out_sums_ref)


def conv_channels_kernel(x_ref, w_ref, mid_ref, inner_ref, outer_ref):
    before, mid, after = tap_columns(nn(w_ref[...], x_ref[...]))
    inner, outer = by_parity(before[:, CELLS - LR :], after[:, :LR])
    inner_ref[...] = inner
    outer_ref[...] = outer
    mid_ref[...] = mid


def whole(x):
    return jnp.sum(jnp.sum(x, axis=0, keepdims=True), axis=1, keepdims=True)


def own_sums(total, sums_ref):
    lane = iota((1, 128), 1)
    row = jnp.zeros((1, 128), F32)
    for k in range(2):
        half = total[GC * k : GC * (k + 1)]
        row = jnp.where(lane == k, whole(half), row)
        row = jnp.where(lane == k + GROUPS, whole(half * half), row)
    sums_ref[...] = jnp.broadcast_to(row[None], sums_ref.shape)


def finish_kernel(mid_ref, inner_ref, outer_ref, cols_ref, own_ref, total_ref, sums_ref):
    right, left = by_parity(inner_ref[...], outer_ref[...])
    total = with_sides(mid_ref[...], left, right)
    total = (own_ref[...].astype(F32) + total + cols_ref[:, 3:4]).astype(BF16)
    total_ref[...] = total
    own_sums(total.astype(F32), sums_ref)


def norm_kernel(which, total_ref, sums_ref, cols_ref, out_ref):
    mean, rstd = moments(sums_ref)
    upper = iota((OC, 1), 0) < GC
    gain = jnp.where(upper, rstd[:, 0:1], rstd[:, 1:2]) * cols_ref[:, 3 * which + 1 : 3 * which + 2]
    shift = cols_ref[:, 3 * which + 2 : 3 * which + 3]
    offset = shift - jnp.where(upper, mean[:, 0:1], mean[:, 1:2]) * gain
    value = total_ref[...].astype(F32) * gain + offset
    if which == 0:
        value = silu(value)
    out_ref[...] = jnp.broadcast_to(value.astype(BF16)[None], out_ref.shape)


def join_kernel(left_ref, right_ref, out_ref, sems):
    count = left_ref.shape[0]
    copies = [
        pltpu.make_async_copy(left_ref, out_ref.at[pl.ds(0, count)], sems.at[0]),
        pltpu.make_async_copy(right_ref, out_ref.at[pl.ds(count, count)], sems.at[1]),
    ]
    for copy in copies:
        copy.start()
    for copy in copies:
        copy.wait()


def attention_kernel(
    x_ref,
    w_ref,
    w_out_ref,
    own_ref,
    far_ref,
    near_hbm,
    part_ref,
    fresh_ref,
    near_ref,
    sem,
):
    chunk = 8
    copy = pltpu.make_async_copy(near_hbm, near_ref, sem)
    copy.start()
    mapped = nn(w_ref[...], x_ref[...])
    queries = jnp.transpose(mapped[:HEAD]).astype(BF16)
    fresh = jnp.transpose(mapped[HEAD:]).astype(BF16)
    queries = (queries.astype(F32) * HEAD ** (-0.5)).astype(BF16)
    queries = jnp.concatenate([queries, jnp.zeros((CELLS, HEAD), BF16)], axis=1)
    order = cell_order()
    fresh_ref[...] = nn(order, fresh).astype(BF16)
    highest = jnp.full((CELLS, 1), -jnp.inf, F32)
    denominator = jnp.zeros((CELLS, 1), F32)
    weighted = jnp.zeros((CELLS, 2 * HEAD), F32)
    for step in range(NS // chunk):
        half, start = divmod(chunk * step, NS // 2)
        if half == 1 and start == 0:
            copy.wait()
        pairs = (far_ref, near_ref)[half][start : start + chunk]
        pairs = pairs.reshape(chunk * CELLS, 2 * HEAD)
        if half == 1 and start == 0:
            pairs = jnp.concatenate([fresh, pairs[CELLS:]], axis=0)
        scores = nt(queries, pairs)
        raised = jnp.maximum(highest, jnp.max(scores, axis=1, keepdims=True))
        factor = jnp.exp(highest - raised)
        weights = jnp.exp(scores - raised)
        denominator = denominator * factor + jnp.sum(weights, axis=1, keepdims=True)
        weighted = weighted * factor + nn(weights.astype(BF16), pairs)
        highest = raised
    attended = nn(order, (weighted / denominator).astype(BF16)).astype(BF16)
    own = nt(order, own_ref[...]).astype(BF16)
    pick = one_hot(iota((OC, C), 1) == iota((OC, C), 0) + lax.axis_index(PROW) * OC, BF16)
    part = nt(attended, w_out_ref[...]) + nn(own, pick)
    part_ref[...] = part.astype(BF16).reshape(part_ref.shape)


def output_kernel(parts_ref, out_ref):
    total = jnp.sum(parts_ref[...].astype(F32), axis=0)
    for r in range(PC):
        out_ref[r] = total[PC * r : PC * (r + 1), :].astype(BF16)


def call(kernel, outs, outer=0, mib=8, space=pltpu.VMEM, scratch=()):
    def run(*args):
        args = list(args)
        for k in range(len(args) - outer, len(args)):
            args[k] = pltpu.with_memory_space_constraint(args[k], pltpu.HBM)
        specs = [pl.BlockSpec(memory_space=pltpu.VMEM)] * (len(args) - outer)
        specs += [pl.BlockSpec(memory_space=pltpu.HBM)] * outer
        return pl.pallas_call(
            kernel,
            out_shape=[
                pltpu.HBM(*out) if space is pltpu.HBM else jax.ShapeDtypeStruct(*out) for out in outs
            ],
            in_specs=specs,
            out_specs=[pl.BlockSpec(memory_space=space)] * len(outs),
            scratch_shapes=list(scratch),
            compiler_params=pltpu.CompilerParams(vmem_limit_bytes=mib * 2**20),
        )(*args)

    return run


def to_every(copies, axis):
    return lax.all_to_all(copies, axis, split_axis=0, concat_axis=0, tiled=True)


def swapped(inner, outer):
    pairs = [(i, j) for i in range(NS) if 0 <= (j := i + 1 if i % 2 else i - 1) < NS]
    outer = lax.ppermute(outer, PCOL, pairs)
    return lax.ppermute(inner, PCOL[-1], [(0, 1), (1, 0)]), outer


def shards(
    latent,
    norm_scale,
    norm_shift,
    time_shift,
    conv_bias,
    conv_one,
    conv_two,
    w_qkv,
    w_out,
    stale_kv,
):
    near = stale_kv.reshape(1, CELLS, 2 * HEAD)
    for step, (axis, bit) in enumerate(HOPS):
        count = lax.axis_size(axis)
        far = lax.ppermute(near, axis, [(i, i ^ bit) for i in range(count)])
        if step < len(HOPS) - 1:
            out = ((2 * near.shape[0], CELLS, 2 * HEAD), BF16)
            (near,) = call(
                join_kernel, [out], space=pltpu.HBM, scratch=[pltpu.SemaphoreType.DMA((2,))]
            )(near, far)
    sums_out = ((NS, 1, 128), F32)
    every = ((NP, OC, CELLS), BF16)
    tile = ((OC, CELLS), F32)
    edge = ((LR, C), BF16)
    (cols,) = call(columns_kernel, [((OC, 128), F32)])(
        norm_scale, norm_shift, conv_bias, time_shift.reshape(1, C)
    )

    def gathered(which, total, sums):
        sums = to_every(sums, PCOL)
        (copies,) = call(functools.partial(norm_kernel, which), [every])(total, sums, cols)
        return to_every(copies, PROW).reshape(C, CELLS)

    (block,) = call(
        pack_kernel,
        [((NP, BLOCK, 128), BF16)],
        outer=2,
        scratch=[
            pltpu.VMEM((PC, PC, C), BF16),
            pltpu.VMEM(w_out.shape, BF16),
            pltpu.SemaphoreType.DMA((2,)),
        ],
    )(latent, w_out)
    block = to_every(block, PROW)
    sums, inner, outer = call(stats_cells_kernel, [sums_out, edge, edge])(block)
    sums = to_every(sums, PCOL)
    inner, outer = swapped(inner, outer)
    (w_part,) = call(
        unpack_kernel,
        [((C, 128), BF16)],
        space=pltpu.HBM,
        scratch=[pltpu.VMEM((C, 128), BF16), pltpu.SemaphoreType.DMA],
    )(block)
    total, sums, own = call(conv_cells_kernel, [tile, sums_out, ((OC, CELLS), BF16)])(
        block,
        sums,
        norm_scale,
        norm_shift,
        conv_one.reshape(9 * OC, C),
        inner,
        outer,
        cols,
    )
    field = gathered(0, total, sums)
    mid, inner, outer = call(
        conv_channels_kernel, [tile, ((OC, LR), F32), ((OC, LR), F32)]
    )(field, conv_two.reshape(9 * OC, C))
    inner, outer = swapped(inner, outer)
    resnet, sums = call(finish_kernel, [((OC, CELLS), BF16), sums_out])(
        mid, inner, outer, cols, own
    )
    field = gathered(1, resnet, sums)
    parts, fresh = call(
        attention_kernel,
        [((NP, NP, C), BF16), ((CELLS, 2 * HEAD), BF16)],
        outer=1,
        mib=16,
        scratch=[pltpu.VMEM((NS // 2, CELLS, 2 * HEAD), BF16), pltpu.SemaphoreType.DMA],
    )(field, w_qkv, w_part, resnet, far, near)
    (out,) = call(output_kernel, [((PC, PC, C), BF16)])(to_every(parts, PROW))
    return out, fresh.reshape(LR, PC, 1, 2 * HEAD)


def solution(mesh):
    torus = Mesh(
        mesh.devices.reshape(2, 8, 4, 4, 2), ("prow_0", "prow_1", "pcol_0", "pcol_1", "pcol_2")
    )
    in_specs = (
        P(PROW, PCOL, None),
        P(),
        P(),
        P(),
        P(),
        P(None, None, PROW, None),
        P(None, None, PROW, None),
        P(PROW, None),
        P(PROW, None),
        P(None, PCOL, PROW, None),
    )
    out_specs = (P(PROW, PCOL, None), P(None, PCOL, PROW, None))

    return jax.shard_map(
        shards, mesh=torus, in_specs=in_specs, out_specs=out_specs, check_vma=False
    )
```
